256 devices in a mesh: energy: 64 (over z, x, y_lo), mom: 4 (over y_hi, core).
Axes of the slice: x: 4, y: 4 (y_hi: 2, y_lo: 2; y = y_hi * 2 + y_lo), z: 8, core: 2. Of those that a mesh axis runs over, the one named last changes fastest.
Arguments:
- green: bfloat16 [4, 128, 16, 2048], P('mom', 'energy'), may hold values from -6 to 6
- coupling: float32 [4, 6, 9, 5, 16], P('mom'), may hold values from -0.12 to 0.12
- gradient: bfloat16 [5, 3, 16, 1024], replicated, may hold values from -1 to 1
- neighbours: int32 [16, 5], replicated, may hold values from 0 to 15, as said below
- offsets: int32 [3], replicated, may hold values from 1 to 4, as said below
Outputs:
- sigma: float32 [128, 16, 2048], P('energy', 'mom')
The draws below stay inside these ranges and needn't reach their ends.
Inputs may be any that keep to these rules, and one draw needn't show every extreme that they name: `neighbours`: each row names 5 different atoms, none of them the row's own atom. `offsets`: one offset is at most 2 and one equals 4.
All inputs are finite; a program needn't handle non-finite values.
Results may differ from the reference program's by a relative error of at most 0.012.
Values may be sent and summed in bfloat16 or wider, within the bound.
A program may use at most 64 MiB of HBM per device.

```python
import jax
import jax.numpy as jnp
from jax import lax

NO = 32
NB = 5
NW = 3
NA = 16
E_DEV = 2
NE = 128
NK = 4


def draw_neighbours(key, part):
    keys = jax.random.split(jax.random.fold_in(key, 11), NA)
    others = jnp.arange(NA - 1, dtype=jnp.int32)
    orders = jax.vmap(lambda single: jax.random.permutation(single, others))(keys)
    atoms = jnp.arange(NA, dtype=jnp.int32)[:, None]
    return ((atoms + 1 + orders[:, :NB]) % NA).astype(jnp.int32)


def draw_offsets(key, part):
    first, second, third = jax.random.split(jax.random.fold_in(key, 23), 3)
    lower = jax.random.randint(first, (1,), 1, E_DEV + 1, dtype=jnp.int32)
    upper = jnp.full((1,), 2 * E_DEV, jnp.int32)
    others = jax.random.randint(second, (NW - 2,), 1, 2 * E_DEV + 1, dtype=jnp.int32)
    values = jnp.concatenate([lower, upper, others], 0)
    return jax.random.permutation(third, values).astype(jnp.int32)


def levels(rng, extent, cuts, low, high):
    def one(axis_at, blocks):
        steps = jax.random.uniform(jax.random.fold_in(jax.random.fold_in(rng, 6), axis_at), (blocks,), jnp.float32, low / len(cuts), high / len(cuts))
        return jnp.repeat(jnp.exp(steps), extent[axis_at] // blocks).reshape((-1,) + (1,) * (len(extent) - axis_at - 1))

    loudness = one(*cuts[0])
    for cut in cuts[1:]:
        loudness = loudness * one(*cut)
    return loudness


def normal_values(rng, dims, width, most, cuts=(), kind=jnp.bfloat16):
    level = levels(rng, dims, cuts, -0.22, 0.18) if cuts else 1.0
    array = jax.random.normal(rng, dims, jnp.float32) * width * level
    return jnp.minimum(jnp.maximum(array, -most), most).astype(kind)


def setup_inputs(seed: int = 0) -> dict:
    key_of = jax.random.split(jax.random.key(seed), 6)
    green = normal_values(key_of[0], (NK, NE, NA, 2 * NO * NO), 1.0, 6.0, ((0, 4), (1, 64)))
    coupling = normal_values(key_of[1], (NK, 2 * NW, 9, NB, NA), 0.02, 0.12, ((0, 4),), jnp.float32)
    gradient = normal_values(key_of[2], (NB, 3, NA, NO * NO), NO ** -0.5, 1.0)
    neighbours = draw_neighbours(jax.random.fold_in(key_of[5], 71), 0)
    offsets = draw_offsets(jax.random.fold_in(key_of[5], 71), 0)
    return {"green": green, "coupling": coupling, "gradient": gradient, "neighbours": neighbours, "offsets": offsets}


def shifted_stack(window, offsets, count, margin):
    pieces = []
    for phonon in range(NW):
        for direction in (1, -1):
            start = (margin - direction * offsets[phonon]).astype(jnp.int32)
            pieces.append(lax.dynamic_slice_in_dim(window, start, count, 0))
    return jnp.stack(pieces, 0)


def sandwich(shifted, weights, gradient, neighbours):
    count = shifted.shape[1]
    natoms = shifted.shape[2]
    blocks = shifted.reshape(2 * NW, count, natoms, 2, NO, NO).astype(jnp.float32)
    derivs_all = gradient.astype(jnp.float32)

    def one_slot(total, slot):
        table = lax.dynamic_index_in_dim(weights, slot, 2, keepdims=False).reshape(2 * NW, 3, 3, natoms)
        derivs = lax.dynamic_index_in_dim(derivs_all, slot, 0, keepdims=False).reshape(3, natoms, NO, NO)
        kernel = jnp.einsum("sija,janl->aslin", table, derivs).astype(jnp.bfloat16)
        kernel = lax.optimization_barrier(kernel).astype(jnp.float32)
        column = lax.dynamic_index_in_dim(neighbours, slot, 1, keepdims=False).astype(jnp.int32)
        gathered = jnp.take(blocks, column, axis=2)
        middle = jnp.einsum("seacml,aslin->aiecmn", gathered, kernel).astype(jnp.bfloat16)
        middle = lax.optimization_barrier(middle).astype(jnp.float32)
        total = total + jnp.einsum("iapm,aiecmn->eacpn", derivs, middle)
        return total, None

    start_total = jnp.zeros((count, natoms, 2, NO, NO), jnp.float32)
    total, _ = lax.scan(one_slot, start_total, jnp.arange(NB, dtype=jnp.int32))
    return total


def reference(green, coupling, gradient, neighbours, offsets):
    margin = 2 * E_DEV
    total = jnp.zeros((NE, NA, 2, NO, NO), jnp.float32)
    for momentum in range(NK):
        padded = jnp.pad(green[momentum], ((margin, margin), (0, 0), (0, 0)))
        shifted = shifted_stack(padded, offsets, NE, margin)
        total = total + sandwich(shifted, coupling[momentum], gradient, neighbours)
    return total.reshape(NE, NA, 2 * NO * NO)
```

```python
import jax
import jax.numpy as jnp
from jax import lax
from jax.experimental import pallas as pl
from jax.experimental.pallas import tpu as pltpu
from jax.sharding import PartitionSpec as P

NO = 32
NB = 5
NW = 3
NA = 16
NS = 2 * NW
ROWS = NB * 3 * NA
MESH = pl.DeviceIdType.MESH
F32 = jnp.float32
BF16 = jnp.bfloat16
NT = (((1,), (1,)), ((), ()))
SHIFTS = (-2, -1, 1, 2)


def lane_group(rows, lanes=128):
    return lax.broadcasted_iota(jnp.int32, (rows, lanes), 1) // NO


def kernel(
    green, coupling, gradient, neighbours, offsets, out,
    own, halo, grad_v, coup_v, near, offs,
    spread, coef, kern, derivs, wide, blocks, sums, send_buf, recv_buf, turned,
    local_sem, halo_send, halo_recv, part_send, part_recv,
):
    n_energy = lax.axis_size("energy")
    energy = lax.axis_index("energy")
    mom = lax.axis_index("mom")

    loads = [
        pltpu.make_async_copy(gradient, grad_v, local_sem.at[0]),
        pltpu.make_async_copy(coupling, coup_v, local_sem.at[1]),
        pltpu.make_async_copy(offsets, offs, local_sem.at[2]),
        pltpu.make_async_copy(green, own, local_sem.at[3]),
        pltpu.make_async_copy(neighbours, near, local_sem.at[4]),
    ]
    for load in loads:
        load.start()

    def inside(by):
        return jnp.logical_and(energy + by >= 0, energy + by < n_energy)

    barrier = pltpu.get_barrier_semaphore()
    for by in SHIFTS:
        @pl.when(inside(by))
        def _():
            pl.semaphore_signal(barrier, inc=1, device_id={"energy": energy + by}, device_id_type=MESH)
    for step in range(1, 4):
        pl.semaphore_signal(barrier, inc=1, device_id={"mom": lax.rem(mom + step, 4)}, device_id_type=MESH)
    expected = 3
    for by in SHIFTS:
        expected = expected + inside(by).astype(jnp.int32)

    loads[0].wait()
    row = lax.broadcasted_iota(jnp.int32, (128, 512), 0)
    col = lax.broadcasted_iota(jnp.int32, (128, 512), 1)
    pick = jnp.where(
        jnp.logical_and(row // NO == col // 128, row % NO == col % NO), 1.0, 0.0
    ).astype(BF16)

    def spread_chunk(chunk, carry):
        part = grad_v[:, pl.ds(pl.multiple_of(chunk * 128, 128), 128)]
        wide_part = jnp.dot(part, pick, preferred_element_type=F32)
        for q in range(4):
            start = pl.multiple_of((chunk * 4 + q) * ROWS, 8)
            spread[pl.ds(start, ROWS), :] = wide_part[:, q * 128 : (q + 1) * 128]
        return carry

    lax.fori_loop(0, 8, spread_chunk, 0)

    pl.semaphore_wait(barrier, expected)

    def halo_copy(slot):
        by = SHIFTS[slot]
        return pltpu.make_async_remote_copy(
            src_ref=green,
            dst_ref=halo.at[3 - slot],
            send_sem=halo_send.at[slot],
            recv_sem=halo_recv.at[3 - slot],
            device_id={"energy": energy + by},
            device_id_type=MESH,
        )

    for slot in range(4):
        @pl.when(inside(SHIFTS[slot]))
        def _():
            halo_copy(slot).start()

    loads[1].wait()
    loads[2].wait()
    group = lane_group(8, 256)
    delta = jnp.where(group < 4, group - 4, group - 3)
    marks = []
    for w in range(NW):
        for u in (1, -1):
            marks.append(jnp.where(delta == u * offs[w], 1.0, 0.0)[:NB])

    def coef_pair(pair, carry):
        tables = [coup_v[s, pair] for s in range(NS)]
        for atom in range(NA):
            total = jnp.zeros((NB, 256), F32)
            for s in range(NS):
                total = total + jnp.broadcast_to(tables[s][:, atom : atom + 1], (NB, 256)) * marks[s]
            coef[atom, pair, :NB, :] = total
        return carry

    lax.fori_loop(0, 9, coef_pair, 0)

    def make_kernels(atom, carry):
        for slot in range(NB):
            d = []
            for j in range(3):
                block = spread[pl.ds((slot * 3 + j) * NA + atom, NO, stride=ROWS), :]
                derivs[atom, slot * 3 + j] = block.astype(BF16)
                d.append(block)
            for i in range(3):
                for half in range(2):
                    total = None
                    for j in range(3):
                        line = coef[atom, 3 * i + j, slot : slot + 1, half * 128 : (half + 1) * 128]
                        term = jnp.broadcast_to(line, (NO, 128)) * d[j]
                        total = term if total is None else total + term
                    kern[atom, slot, i * NO : (i + 1) * NO, half * 128 : (half + 1) * 128] = total.astype(BF16)
        return carry

    lax.fori_loop(0, NA, make_kernels, 0)

    def place(block, ref, ref_at):
        def chunk_step(chunk, carry):
            for eps in range(2):
                lanes = pl.ds(pl.multiple_of(chunk * 128, 128), 128)
                index = (eps, slice(None), lanes) if ref_at is None else (ref_at, eps, slice(None), lanes)
                tile = ref[index].astype(F32)
                turns = [tile] + [pltpu.roll(tile, NO * k, 1) for k in range(1, 4)]
                for e in range(2):
                    diff = e - (2 * block + eps)
                    if diff == 0 or abs(diff) > 4:
                        continue
                    k = diff + 4 if diff < 0 else diff + 3
                    half, at = k // 4, k % 4
                    for q in range(4):
                        start = pl.multiple_of((chunk * 4 + q) * NA, NA)
                        wide[e * 2 + half, pl.ds(start, NA), at * NO : (at + 1) * NO] = turns[(at - q) % 4][
                            :, at * NO : (at + 1) * NO
                        ]
            return carry

        lax.fori_loop(0, 16, chunk_step, 0)

    loads[3].wait()
    place(0, own, None)
    for slot in (1, 2, 0, 3):
        @pl.when(inside(SHIFTS[slot]))
        def _():
            halo_copy(3 - slot).wait_recv()

        @pl.when(jnp.logical_not(inside(SHIFTS[slot])))
        def _():
            halo[slot] = jnp.zeros(halo.shape[1:], BF16)

        place(SHIFTS[slot], halo, slot)

    def gather_atom(atom, carry):
        for e in range(2):
            for half in range(2):
                part = wide[e * 2 + half, pl.ds(atom, 2 * NO, stride=NA), :]
                blocks[atom, e * 64 : (e + 1) * 64, half * 128 : (half + 1) * 128] = part.astype(BF16)
        return carry

    lax.fori_loop(0, NA, gather_atom, 0)
    loads[4].wait()

    group = lane_group(NO)
    masks = [group == g for g in range(4)]

    def one_atom(atom):
        lefts, rights = [], []
        for slot in range(NB):
            middle = lax.dot_general(
                kern[atom, slot], blocks[near[atom, slot]], NT, preferred_element_type=F32
            ).astype(BF16)
            for i in range(3):
                lefts.append(middle[i * NO : (i + 1) * NO, :])
                block = derivs[atom, slot * 3 + i]
                zero = jnp.zeros_like(block)
                rights.append(jnp.concatenate([jnp.where(mask, block, zero) for mask in masks], axis=0))
        left = jnp.concatenate(lefts, axis=1)
        right = jnp.concatenate(rights, axis=1)
        return lax.dot_general(left, right, NT, preferred_element_type=F32)

    def target(step):
        high = lax.rem(mom // 2 + 1 - step // 2, 2)
        low = lax.rem(mom + (step + 1) // 2, 2)
        return 2 * high + low

    def part_copy(step):
        return pltpu.make_async_remote_copy(
            src_ref=send_buf.at[step],
            dst_ref=recv_buf.at[step],
            send_sem=part_send.at[step],
            recv_sem=part_recv.at[step],
            device_id={"mom": target(step)},
            device_id_type=MESH,
        )

    def part_step(step, carry):
        for at in range(4):
            send_buf[step, at] = one_atom(4 * target(step) + at).astype(BF16)
        part_copy(step).start()
        return carry

    lax.fori_loop(0, 3, part_step, 0)
    for at in range(4):
        sums[at] = one_atom(4 * mom + at)

    for step in range(3):
        part_copy(step).wait_recv()
    for at in range(4):
        total = sums[at]
        for step in range(3):
            total = total + recv_buf[step, at].astype(F32)
        turned[at * 128 : (at + 1) * 128, :] = jnp.concatenate([total] * 4, axis=0).T
    for e in range(2):
        for c in range(2):
            for high in range(8):
                value = None
                for low in range(4):
                    line = turned[pl.ds((e * 2 + c) * 32 + high * 4 + low, 4, stride=128), :]
                    value = line if value is None else jnp.where(masks[low][:4], line, value)
                start = (c * 8 + high) * 128
                out[e, :, start : start + 128] = value

    for slot in range(4):
        @pl.when(inside(SHIFTS[slot]))
        def _():
            halo_copy(slot).wait_send()
    for step in range(3):
        part_copy(step).wait_send()


def body(green, coupling, gradient, neighbours, offsets):
    count, natoms = green.shape[1], green.shape[2]
    anywhere = pl.BlockSpec(memory_space=pl.ANY)
    vmem = pltpu.VMEM
    dma = pltpu.SemaphoreType.DMA
    return pl.pallas_call(
        kernel,
        out_shape=jax.ShapeDtypeStruct((count, natoms // 4, 2 * NO * NO), F32),
        in_specs=[anywhere] * 5,
        out_specs=pl.BlockSpec(memory_space=vmem),
        scratch_shapes=[
            vmem((2, NA, 2048), BF16),
            vmem((4, 2, NA, 2048), BF16),
            vmem((ROWS, 1024), BF16),
            vmem((NS, 9, NB, NA), F32),
            pltpu.SMEM((NA, NB), jnp.int32),
            pltpu.SMEM((NW,), jnp.int32),
            vmem((NO * ROWS, 128), F32),
            vmem((NA, 9, 8, 256), F32),
            vmem((NA, NB, 96, 256), BF16),
            vmem((NA, NB * 3, NO, 128), BF16),
            vmem((4, 64 * NA, 128), F32),
            vmem((NA, 128, 256), BF16),
            vmem((4, NO, 128), F32),
            vmem((3, 4, NO, 128), BF16),
            vmem((3, 4, NO, 128), BF16),
            vmem((512, 128), F32),
            dma((5,)),
            dma((4,)),
            dma((4,)),
            dma((3,)),
            dma((3,)),
        ],
        compiler_params=pltpu.CompilerParams(collective_id=0, has_side_effects=True),
    )(green[0], coupling[0], gradient.reshape(ROWS, NO * NO), neighbours, offsets)


def solution(mesh):
    in_specs = (P("mom", "energy", None, None), P("mom", None, None, None, None), P(), P(), P())
    out_specs = P("energy", "mom", None)
    return jax.shard_map(body, mesh=mesh, in_specs=in_specs, out_specs=out_specs, check_vma=False)
```

```python
import jax
import jax.numpy as jnp
from jax import lax
from jax.experimental import pallas as pl
from jax.experimental.pallas import tpu as pltpu
from jax.sharding import PartitionSpec as P

NO = 32
NB = 5
NW = 3
NA = 16
NS = 2 * NW
ROWS = NB * 3 * NA
MESH = pl.DeviceIdType.MESH
F32 = jnp.float32
BF16 = jnp.bfloat16
NT = (((1,), (1,)), ((), ()))
SHIFTS = (-2, -1, 1, 2)


def lane_group(rows, lanes=128):
    return lax.broadcasted_iota(jnp.int32, (rows, lanes), 1) // NO


def kernel(
    green, coupling, gradient, neighbours, offsets, out,
    own, halo, grad_v, coup_v, near, offs,
    spread, coef, kern, derivs, wide, blocks, sums, send_buf, recv_buf, turned,
    local_sem, halo_send, halo_recv, part_send, part_recv,
):
    n_energy = lax.axis_size("energy")
    energy = lax.axis_index("energy")
    mom = lax.axis_index("mom")

    loads = [
        pltpu.make_async_copy(gradient, grad_v, local_sem.at[0]),
        pltpu.make_async_copy(coupling, coup_v, local_sem.at[1]),
        pltpu.make_async_copy(offsets, offs, local_sem.at[2]),
        pltpu.make_async_copy(green, own, local_sem.at[3]),
        pltpu.make_async_copy(neighbours, near, local_sem.at[4]),
    ]
    for load in loads:
        load.start()

    def inside(by):
        return jnp.logical_and(energy + by >= 0, energy + by < n_energy)

    barrier = pltpu.get_barrier_semaphore()
    for by in SHIFTS:
        @pl.when(inside(by))
        def _():
            pl.semaphore_signal(barrier, inc=1, device_id={"energy": energy + by}, device_id_type=MESH)
    for step in range(1, 4):
        pl.semaphore_signal(barrier, inc=1, device_id={"mom": lax.rem(mom + step, 4)}, device_id_type=MESH)
    expected = 3
    for by in SHIFTS:
        expected = expected + inside(by).astype(jnp.int32)

    loads[0].wait()
    row = lax.broadcasted_iota(jnp.int32, (128, 512), 0)
    col = lax.broadcasted_iota(jnp.int32, (128, 512), 1)
    pick = jnp.where(
        jnp.logical_and(row // NO == col // 128, row % NO == col % NO), 1.0, 0.0
    ).astype(BF16)

    def spread_chunk(chunk, carry):
        part = grad_v[:, pl.ds(pl.multiple_of(chunk * 128, 128), 128)]
        wide_part = jnp.dot(part, pick, preferred_element_type=F32)
        for q in range(4):
            start = pl.multiple_of((chunk * 4 + q) * ROWS, 8)
            spread[pl.ds(start, ROWS), :] = wide_part[:, q * 128 : (q + 1) * 128]
        return carry

    lax.fori_loop(0, 8, spread_chunk, 0)

    pl.semaphore_wait(barrier, expected)

    def halo_copy(slot):
        by = SHIFTS[slot]
        return pltpu.make_async_remote_copy(
            src_ref=green,
            dst_ref=halo.at[3 - slot],
            send_sem=halo_send.at[slot],
            recv_sem=halo_recv.at[3 - slot],
            device_id={"energy": energy + by},
            device_id_type=MESH,
        )

    for slot in range(4):
        @pl.when(inside(SHIFTS[slot]))
        def _():
            halo_copy(slot).start()

    loads[1].wait()
    loads[2].wait()
    group = lane_group(8, 256)
    delta = jnp.where(group < 4, group - 4, group - 3)
    marks = []
    for w in range(NW):
        for u in (1, -1):
            marks.append(jnp.where(delta == u * offs[w], 1.0, 0.0)[:NB])

    def coef_pair(pair, carry):
        tables = [coup_v[s, pair, :, 0, :] for s in range(NS)]
        for atom in range(NA):
            total = jnp.zeros((NB, 256), F32)
            for s in range(NS):
                total = total + jnp.broadcast_to(tables[s][:, atom : atom + 1], (NB, 256)) * marks[s]
            coef[atom, pair, :NB, :] = total
        return carry

    lax.fori_loop(0, 9, coef_pair, 0)

    def make_kernels(atom, carry):
        for slot in range(NB):
            d = []
            for j in range(3):
                block = spread[pl.ds((slot * 3 + j) * NA + atom, NO, stride=ROWS), :]
                derivs[atom, slot * 3 + j] = block.astype(BF16)
                d.append(block)
            for i in range(3):
                for half in range(2):
                    total = None
                    for j in range(3):
                        line = coef[atom, 3 * i + j, slot : slot + 1, half * 128 : (half + 1) * 128]
                        term = jnp.broadcast_to(line, (NO, 128)) * d[j]
                        total = term if total is None else total + term
                    kern[atom, slot, i * NO : (i + 1) * NO, half * 128 : (half + 1) * 128] = total.astype(BF16)
        return carry

    lax.fori_loop(0, NA, make_kernels, 0)

    def place(block, ref, ref_at):
        def chunk_step(chunk, carry):
            for eps in range(2):
                lanes = pl.ds(pl.multiple_of(chunk * 128, 128), 128)
                index = (eps, slice(None), lanes) if ref_at is None else (ref_at, eps, slice(None), lanes)
                tile = ref[index].astype(F32)
                turns = [tile] + [pltpu.roll(tile, NO * k, 1) for k in range(1, 4)]
                for e in range(2):
                    diff = e - (2 * block + eps)
                    if diff == 0 or abs(diff) > 4:
                        continue
                    k = diff + 4 if diff < 0 else diff + 3
                    half, at = k // 4, k % 4
                    for q in range(4):
                        start = pl.multiple_of((chunk * 4 + q) * NA, NA)
                        wide[e * 2 + half, pl.ds(start, NA), at * NO : (at + 1) * NO] = turns[(at - q) % 4][
                            :, at * NO : (at + 1) * NO
                        ]
            return carry

        lax.fori_loop(0, 16, chunk_step, 0)

    loads[3].wait()
    place(0, own, None)
    for slot in (1, 2, 0, 3):
        @pl.when(inside(SHIFTS[slot]))
        def _():
            halo_copy(3 - slot).wait_recv()

        @pl.when(jnp.logical_not(inside(SHIFTS[slot])))
        def _():
            halo[slot] = jnp.zeros(halo.shape[1:], BF16)

        place(SHIFTS[slot], halo, slot)

    def gather_atom(atom, carry):
        for e in range(2):
            for half in range(2):
                part = wide[e * 2 + half, pl.ds(atom, 2 * NO, stride=NA), :]
                blocks[atom, e * 64 : (e + 1) * 64, half * 128 : (half + 1) * 128] = part.astype(BF16)
        return carry

    lax.fori_loop(0, NA, gather_atom, 0)
    loads[4].wait()

    group = lane_group(NO)
    masks = [group == g for g in range(4)]

    def one_atom(atom):
        lefts, rights = [], []
        for slot in range(NB):
            middle = lax.dot_general(
                kern[atom, slot], blocks[near[slot, atom]], NT, preferred_element_type=F32
            ).astype(BF16)
            for i in range(3):
                lefts.append(middle[i * NO : (i + 1) * NO, :])
                block = derivs[atom, slot * 3 + i]
                zero = jnp.zeros_like(block)
                rights.append(jnp.concatenate([jnp.where(mask, block, zero) for mask in masks], axis=0))
        left = jnp.concatenate(lefts, axis=1)
        right = jnp.concatenate(rights, axis=1)
        return lax.dot_general(left, right, NT, preferred_element_type=F32)

    def target(step):
        high = lax.rem(mom // 2 + 1 - step // 2, 2)
        low = lax.rem(mom + (step + 1) // 2, 2)
        return 2 * high + low

    def part_copy(step):
        return pltpu.make_async_remote_copy(
            src_ref=send_buf.at[step],
            dst_ref=recv_buf.at[step],
            send_sem=part_send.at[step],
            recv_sem=part_recv.at[step],
            device_id={"mom": target(step)},
            device_id_type=MESH,
        )

    def part_step(step, carry):
        for at in range(4):
            send_buf[step, at] = one_atom(4 * target(step) + at).astype(BF16)
        part_copy(step).start()
        return carry

    lax.fori_loop(0, 3, part_step, 0)
    for at in range(4):
        sums[at] = one_atom(4 * mom + at)

    for step in range(3):
        part_copy(step).wait_recv()
    for at in range(4):
        total = sums[at]
        for step in range(3):
            total = total + recv_buf[step, at].astype(F32)
        turned[at * 128 : (at + 1) * 128, :] = jnp.concatenate([total] * 4, axis=0).T
    for e in range(2):
        for c in range(2):
            for high in range(8):
                value = None
                for low in range(4):
                    line = turned[pl.ds((e * 2 + c) * 32 + high * 4 + low, 4, stride=128), :]
                    value = line if value is None else jnp.where(masks[low][:4], line, value)
                start = (c * 8 + high) * 128
                out[e, :, start : start + 128] = value

    for slot in range(4):
        @pl.when(inside(SHIFTS[slot]))
        def _():
            halo_copy(slot).wait_send()
    for step in range(3):
        part_copy(step).wait_send()


def body(green, coupling, gradient, neighbours, offsets):
    count, natoms = green.shape[1], green.shape[2]
    anywhere = pl.BlockSpec(memory_space=pl.ANY)
    vmem = pltpu.VMEM
    dma = pltpu.SemaphoreType.DMA
    return pl.pallas_call(
        kernel,
        out_shape=jax.ShapeDtypeStruct((count, natoms // 4, 2 * NO * NO), F32),
        in_specs=[anywhere] * 5,
        out_specs=pl.BlockSpec(memory_space=vmem),
        scratch_shapes=[
            vmem((2, NA, 2048), BF16),
            vmem((4, 2, NA, 2048), BF16),
            vmem((ROWS, 1024), BF16),
            vmem((NS, 9, NB, 1, NA), F32),
            pltpu.SMEM((NB, NA), jnp.int32),
            pltpu.SMEM((NW,), jnp.int32),
            vmem((NO * ROWS, 128), F32),
            vmem((NA, 9, 8, 256), F32),
            vmem((NA, NB, 96, 256), BF16),
            vmem((NA, NB * 3, NO, 128), BF16),
            vmem((4, 64 * NA, 128), F32),
            vmem((NA, 128, 256), BF16),
            vmem((4, NO, 128), F32),
            vmem((3, 4, NO, 128), BF16),
            vmem((3, 4, NO, 128), BF16),
            vmem((512, 128), F32),
            dma((5,)),
            dma((4,)),
            dma((4,)),
            dma((3,)),
            dma((3,)),
        ],
        compiler_params=pltpu.CompilerParams(collective_id=0, has_side_effects=True),
    )(
        green[0],
        coupling.reshape(NS, 9, NB, 1, NA),
        gradient.reshape(ROWS, NO * NO),
        neighbours.T,
        offsets,
    )


def solution(mesh):
    in_specs = (P("mom", "energy", None, None), P("mom", None, None, None, None), P(), P(), P())
    out_specs = P("energy", "mom", None)
    return jax.shard_map(body, mesh=mesh, in_specs=in_specs, out_specs=out_specs, check_vma=False)
```

```python
import jax
import jax.numpy as jnp
from jax import lax
from jax.experimental import pallas as pl
from jax.experimental.pallas import tpu as pltpu
from jax.sharding import PartitionSpec as P

NO = 32
NB = 5
NW = 3
NA = 16
NS = 2 * NW
ROWS = NB * 3 * NA
STEP = 68
GAP = 20
MESH = pl.DeviceIdType.MESH
F32 = jnp.float32
BF16 = jnp.bfloat16
SHIFTS = (-2, -1, 1, 2)


def lane_group(rows, lanes=128):
    return lax.broadcasted_iota(jnp.int32, (rows, lanes), 1) // NO


def kernel(
    green, coupling, gradient, neighbours, offsets, out,
    own, halo, grad_v, coup_v, near, offs,
    coup_rows, spread, coef, flipped, kern, derivs, wide, blocks, sums, send_buf, recv_buf, turned,
    local_sem, halo_send, halo_recv, part_send, part_recv,
):
    n_energy = lax.axis_size("energy")
    energy = lax.axis_index("energy")
    mom = lax.axis_index("mom")

    loads = [
        pltpu.make_async_copy(gradient, grad_v, local_sem.at[0]),
        pltpu.make_async_copy(coupling, coup_v, local_sem.at[1]),
        pltpu.make_async_copy(offsets, offs, local_sem.at[2]),
        pltpu.make_async_copy(green, own, local_sem.at[3]),
        pltpu.make_async_copy(neighbours, near, local_sem.at[4]),
    ]
    for load in loads:
        load.start()

    def inside(by):
        return jnp.logical_and(energy + by >= 0, energy + by < n_energy)

    barrier = pltpu.get_barrier_semaphore()
    for by in SHIFTS:
        @pl.when(inside(by))
        def _():
            pl.semaphore_signal(barrier, inc=1, device_id={"energy": energy + by}, device_id_type=MESH)
    for step in range(1, 4):
        pl.semaphore_signal(barrier, inc=1, device_id={"mom": lax.rem(mom + step, 4)}, device_id_type=MESH)
    expected = 3
    for by in SHIFTS:
        expected = expected + inside(by).astype(jnp.int32)

    col = lax.broadcasted_iota(jnp.int32, (1, 512), 1)
    wanted = (col // NO) % 4 * 128 + col // 128 * NO + col % NO
    rows = lax.broadcasted_iota(jnp.int32, (512, 512), 0)
    pick = jnp.where(rows == wanted, 1.0, 0.0).astype(BF16)
    loads[0].wait()
    lines = []
    for chunk in range(8):
        tiles = []
        for g in range(4):
            parts = []
            for tile in range(4):
                block = 4 * tile + g
                if block < 3 * NB:
                    parts.append(grad_v[block * NA : (block + 1) * NA, chunk * 128 : (chunk + 1) * 128])
                else:
                    parts.append(jnp.zeros((NA, 128), BF16))
            tiles.append(jnp.concatenate(parts, axis=0))
        lines.append(jnp.concatenate(tiles, axis=1))
    packed = jnp.dot(jnp.concatenate(lines, axis=0), pick, preferred_element_type=F32)
    for chunk in range(8):
        for q in range(4):
            start = (chunk * 4 + q) * STEP
            spread[start : start + 64, :] = packed[chunk * 64 : (chunk + 1) * 64, q * 128 : (q + 1) * 128]

    pl.semaphore_wait(barrier, expected)

    def halo_copy(slot):
        by = SHIFTS[slot]
        return pltpu.make_async_remote_copy(
            src_ref=green,
            dst_ref=halo.at[3 - slot],
            send_sem=halo_send.at[slot],
            recv_sem=halo_recv.at[3 - slot],
            device_id={"energy": energy + by},
            device_id_type=MESH,
        )

    for slot in range(4):
        @pl.when(inside(SHIFTS[slot]))
        def _():
            halo_copy(slot).start()

    loads[1].wait()
    loads[2].wait()

    def coef_rows(pair, carry):
        for slot in range(NB):
            coup_rows[pair, slot : slot + 1, :NA] = coup_v[pair, slot]
        return carry

    lax.fori_loop(0, NS * 9, coef_rows, 0)
    group8 = lane_group(8)
    weights = [
        [jnp.broadcast_to(jnp.where(offs[w] == size, 1.0, 0.0), (8, 128)) for w in range(NW)] for size in range(1, 5)
    ]

    def coef_step(j, carry):
        tables = [[coup_rows[s * 9 + 3 * i + j] for i in range(3)] for s in range(NS)]
        for atom in range(NA):
            terms = []
            for s in range(NS):
                first, second, third = [
                    jnp.broadcast_to(tables[s][i][:, atom : atom + 1], (8, 128)) for i in range(3)
                ]
                terms.append(jnp.where(group8 == 0, first, jnp.where(group8 == 1, second, third)))
            for size in range(1, 5):
                for g in range(2):
                    k = size + 3 if g == 0 else 4 - size
                    total = None
                    for w in range(NW):
                        term = weights[size - 1][w] * terms[2 * w + g]
                        total = term if total is None else total + term
                    coef[atom, k * 3 + j] = total
        return carry

    lax.fori_loop(0, 3, coef_step, 0)

    def make_kernels(atom, carry):
        for tile in range(4):
            block = spread[pl.ds(tile * NA + atom, NO, stride=STEP), :]
            derivs[atom, :, tile * 128 : (tile + 1) * 128] = block.astype(BF16)
            flipped[tile * 128 : (tile + 1) * 128, :] = jnp.concatenate([block] * 4, axis=0).T
        for slot in range(NB):
            d = [flipped[(slot * 3 + j) * NO : (slot * 3 + j + 1) * NO, :] for j in range(3)]
            for k in range(8):
                total = None
                for j in range(3):
                    line = coef[atom, k * 3 + j, slot : slot + 1, :]
                    term = jnp.broadcast_to(line, (NO, 128)) * d[j]
                    total = term if total is None else total + term
                kern[atom, slot, k * NO : (k + 1) * NO, :] = total.astype(BF16)
        return carry

    lax.fori_loop(0, NA, make_kernels, 0)

    def place(block, ref, ref_at):
        def chunk_step(chunk, carry):
            for eps in range(2):
                lanes = pl.ds(pl.multiple_of(chunk * 128, 128), 128)
                index = (eps, slice(None), lanes) if ref_at is None else (ref_at, eps, slice(None), lanes)
                tile = ref[index].astype(F32)
                turns = [tile] + [pltpu.roll(tile, NO * k, 1) for k in range(1, 4)]
                for e in range(2):
                    diff = e - (2 * block + eps)
                    if diff == 0 or abs(diff) > 4:
                        continue
                    k = diff + 4 if diff < 0 else diff + 3
                    half, at = k // 4, k % 4
                    for q in range(4):
                        start = pl.multiple_of((chunk * 4 + q) * GAP, 4)
                        wide[e * 2 + half, pl.ds(start, NA), at * NO : (at + 1) * NO] = turns[(at - q) % 4][
                            :, at * NO : (at + 1) * NO
                        ]
            return carry

        lax.fori_loop(0, 16, chunk_step, 0)

    loads[3].wait()
    place(0, own, None)
    for slot in (1, 2, 0, 3):
        @pl.when(inside(SHIFTS[slot]))
        def _():
            halo_copy(3 - slot).wait_recv()

        @pl.when(jnp.logical_not(inside(SHIFTS[slot])))
        def _():
            halo[slot] = jnp.zeros(halo.shape[1:], BF16)

        place(SHIFTS[slot], halo, slot)

    def gather_atom(atom, carry):
        for e in range(2):
            for half in range(2):
                part = wide[e * 2 + half, pl.ds(atom, 2 * NO, stride=GAP), :]
                blocks[atom, e * 64 : (e + 1) * 64, half * 128 : (half + 1) * 128] = part.astype(BF16)
        return carry

    lax.fori_loop(0, NA, gather_atom, 0)
    loads[4].wait()

    group = lane_group(NO)
    masks = [group == g for g in range(4)]

    def one_atom(atom):
        stack = []
        for slot in range(NB):
            middle = jnp.dot(blocks[near[slot, atom]], kern[atom, slot], preferred_element_type=F32)
            parts = [middle[g * NO : (g + 1) * NO, :] for g in range(4)]
            for i in range(3):
                value = None
                for g in range(4):
                    turn = (g - i) % 4
                    part = pltpu.roll(parts[g], NO * turn, 1) if turn else parts[g]
                    value = part if value is None else jnp.where(masks[g], part, value)
                stack.append(value.astype(BF16))
        stack.append(jnp.zeros((NO, 128), BF16))
        return jnp.dot(derivs[atom], jnp.concatenate(stack, axis=0), preferred_element_type=F32)

    def target(step):
        high = lax.rem(mom // 2 + 1 - step // 2, 2)
        low = lax.rem(mom + (step + 1) // 2, 2)
        return 2 * high + low

    def part_copy(step):
        return pltpu.make_async_remote_copy(
            src_ref=send_buf.at[step],
            dst_ref=recv_buf.at[step],
            send_sem=part_send.at[step],
            recv_sem=part_recv.at[step],
            device_id={"mom": target(step)},
            device_id_type=MESH,
        )

    def part_step(step, carry):
        for at in range(4):
            send_buf[step, at] = one_atom(4 * target(step) + at).astype(BF16)
        part_copy(step).start()
        return carry

    lax.fori_loop(0, 3, part_step, 0)
    for at in range(4):
        sums[at] = one_atom(4 * mom + at)

    for step in range(3):
        part_copy(step).wait_recv()
    for at in range(4):
        total = sums[at]
        for step in range(3):
            total = total + recv_buf[step, at].astype(F32)
        for turn in range(4):
            turned[turn, at * 36 : at * 36 + NO, :] = pltpu.roll(total, NO * turn, 1) if turn else total
    for g in range(4):
        for high in range(8):
            value = None
            for low in range(4):
                line = turned[(low - g) % 4, pl.ds(high * 4 + low, 4, stride=36), :]
                value = line if value is None else jnp.where(masks[low][:4], line, value)
            start = (g % 2 * 8 + high) * 128
            out[g // 2, :, start : start + 128] = value

    for slot in range(4):
        @pl.when(inside(SHIFTS[slot]))
        def _():
            halo_copy(slot).wait_send()
    for step in range(3):
        part_copy(step).wait_send()


def body(green, coupling, gradient, neighbours, offsets):
    count, natoms = green.shape[1], green.shape[2]
    anywhere = pl.BlockSpec(memory_space=pl.ANY)
    vmem = pltpu.VMEM
    dma = pltpu.SemaphoreType.DMA
    return pl.pallas_call(
        kernel,
        out_shape=jax.ShapeDtypeStruct((count, natoms // 4, 2 * NO * NO), F32),
        in_specs=[anywhere] * 5,
        out_specs=pl.BlockSpec(memory_space=vmem),
        scratch_shapes=[
            vmem((2, NA, 2048), BF16),
            vmem((4, 2, NA, 2048), BF16),
            vmem((ROWS, 1024), BF16),
            vmem((NS * 9, NB, 1, NA), F32),
            pltpu.SMEM((NB, NA), jnp.int32),
            pltpu.SMEM((NW,), jnp.int32),
            vmem((NS * 9, 8, 128), F32),
            vmem((NO * STEP, 128), F32),
            vmem((NA, 24, 8, 128), F32),
            vmem((512, 128), F32),
            vmem((NA, NB, 256, 128), BF16),
            vmem((NA, NO, 512), BF16),
            vmem((4, 64 * GAP, 128), F32),
            vmem((NA, 128, 256), BF16),
            vmem((4, NO, 128), F32),
            vmem((3, 4, NO, 128), BF16),
            vmem((3, 4, NO, 128), BF16),
            vmem((4, 4 * 36, 128), F32),
            dma((5,)),
            dma((4,)),
            dma((4,)),
            dma((3,)),
            dma((3,)),
        ],
        compiler_params=pltpu.CompilerParams(collective_id=0, has_side_effects=True),
    )(
        green[0],
        coupling.reshape(NS * 9, NB, 1, NA),
        gradient.reshape(ROWS, NO * NO),
        neighbours.T,
        offsets,
    )


def solution(mesh):
    in_specs = (P("mom", "energy", None, None), P("mom", None, None, None, None), P(), P(), P())
    out_specs = P("energy", "mom", None)
    return jax.shard_map(body, mesh=mesh, in_specs=in_specs, out_specs=out_specs, check_vma=False)
```

```python
import jax
import jax.numpy as jnp
from jax import lax
from jax.experimental import pallas as pl
from jax.experimental.pallas import tpu as pltpu
from jax.sharding import PartitionSpec as P

NO = 32
NB = 5
NW = 3
NA = 16
NS = 2 * NW
ROWS = NB * 3 * NA
STEP = 68
GAP = 20
MESH = pl.DeviceIdType.MESH
F32 = jnp.float32
BF16 = jnp.bfloat16
SHIFTS = (-2, -1, 1, 2)


def lane_group(rows, lanes=128):
    return lax.broadcasted_iota(jnp.int32, (rows, lanes), 1) // NO


def kernel(
    green, coupling, gradient, neighbours, offsets, out,
    own, halo, grad_v, coup_v, near, offs,
    coup_rows, spread, coef, flipped, kern, derivs, wide, blocks, send_buf, recv_buf, turned,
    local_sem, halo_send, halo_recv, part_send, part_recv,
):
    n_energy = lax.axis_size("energy")
    energy = lax.axis_index("energy")
    mom = lax.axis_index("mom")

    loads = [
        pltpu.make_async_copy(gradient, grad_v, local_sem.at[0]),
        pltpu.make_async_copy(coupling, coup_v, local_sem.at[1]),
        pltpu.make_async_copy(offsets, offs, local_sem.at[2]),
        pltpu.make_async_copy(green, own, local_sem.at[3]),
        pltpu.make_async_copy(neighbours, near, local_sem.at[4]),
    ]
    for load in loads:
        load.start()

    def inside(by):
        return jnp.logical_and(energy + by >= 0, energy + by < n_energy)

    barrier = pltpu.get_barrier_semaphore()
    for by in SHIFTS:
        @pl.when(inside(by))
        def _():
            pl.semaphore_signal(barrier, inc=1, device_id={"energy": energy + by}, device_id_type=MESH)
    for step in range(1, 4):
        pl.semaphore_signal(barrier, inc=1, device_id={"mom": lax.rem(mom + step, 4)}, device_id_type=MESH)
    expected = 3
    for by in SHIFTS:
        expected = expected + inside(by).astype(jnp.int32)

    pl.semaphore_wait(barrier, expected)

    def halo_copy(slot):
        by = SHIFTS[slot]
        return pltpu.make_async_remote_copy(
            src_ref=green,
            dst_ref=halo.at[3 - slot],
            send_sem=halo_send.at[slot],
            recv_sem=halo_recv.at[3 - slot],
            device_id={"energy": energy + by},
            device_id_type=MESH,
        )

    for slot in range(4):
        @pl.when(inside(SHIFTS[slot]))
        def _():
            halo_copy(slot).start()

    col = lax.broadcasted_iota(jnp.int32, (1, 512), 1)
    wanted = (col // NO) % 4 * 128 + col // 128 * NO + col % NO
    rows = lax.broadcasted_iota(jnp.int32, (512, 512), 0)
    pick = jnp.where(rows == wanted, 1.0, 0.0).astype(BF16)
    loads[0].wait()
    lines = []
    for chunk in range(8):
        tiles = []
        for g in range(4):
            parts = []
            for tile in range(4):
                block = 4 * tile + g
                if block < 3 * NB:
                    parts.append(grad_v[block * NA : (block + 1) * NA, chunk * 128 : (chunk + 1) * 128])
                else:
                    parts.append(jnp.zeros((NA, 128), BF16))
            tiles.append(jnp.concatenate(parts, axis=0))
        lines.append(jnp.concatenate(tiles, axis=1))
    packed = jnp.dot(jnp.concatenate(lines, axis=0), pick, preferred_element_type=F32)
    for chunk in range(8):
        for q in range(4):
            start = (chunk * 4 + q) * STEP
            spread[start : start + 64, :] = packed[chunk * 64 : (chunk + 1) * 64, q * 128 : (q + 1) * 128]

    loads[1].wait()
    loads[2].wait()

    for pair in range(NS * 9):
        for slot in range(NB):
            coup_rows[pair, slot : slot + 1, :NA] = coup_v[pair, slot]
    group8 = lane_group(8)
    weights = [
        [jnp.broadcast_to(jnp.where(offs[w] == size, 1.0, 0.0), (8, 128)) for w in range(NW)] for size in range(1, 5)
    ]

    def coef_step(j, carry):
        tables = [[coup_rows[s * 9 + 3 * i + j] for i in range(3)] for s in range(NS)]
        for atom in range(NA):
            terms = []
            for s in range(NS):
                first, second, third = [
                    jnp.broadcast_to(tables[s][i][:, atom : atom + 1], (8, 128)) for i in range(3)
                ]
                terms.append(jnp.where(group8 == 0, first, jnp.where(group8 == 1, second, third)))
            for size in range(1, 5):
                for g in range(2):
                    k = 4 * g + size - 1
                    total = None
                    for w in range(NW):
                        term = weights[size - 1][w] * terms[2 * w + g]
                        total = term if total is None else total + term
                    coef[atom, k * 3 + j] = total
        return carry

    lax.fori_loop(0, 3, coef_step, 0)

    def make_kernels(atom, carry):
        for tile in range(4):
            block = spread[pl.ds(tile * NA + atom, NO, stride=STEP), :]
            derivs[atom, :, tile * 128 : (tile + 1) * 128] = block.astype(BF16)
            flipped[tile * 128 : (tile + 1) * 128, :] = jnp.concatenate([block] * 4, axis=0).T
        for slot in range(NB):
            d = [flipped[(slot * 3 + j) * NO : (slot * 3 + j + 1) * NO, :] for j in range(3)]
            for k in range(8):
                total = None
                for j in range(3):
                    line = coef[atom, k * 3 + j, slot : slot + 1, :]
                    term = jnp.broadcast_to(line, (NO, 128)) * d[j]
                    total = term if total is None else total + term
                kern[atom, slot, k * NO : (k + 1) * NO, :] = total.astype(BF16)
        return carry

    lax.fori_loop(0, NA, make_kernels, 0)

    group16 = lane_group(NA)

    def place(block, load):
        def chunk_step(chunk, carry):
            turns = []
            for eps in range(2):
                tile = load(eps, pl.ds(pl.multiple_of(chunk * 128, 128), 128)).astype(F32)
                turns.append([tile] + [pltpu.roll(tile, NO * k, 1) for k in range(1, 4)])
            for e in range(2):
                for half in range(2):
                    found = {}
                    for eps in range(2):
                        diff = (e - (2 * block + eps)) * (1 - 2 * half)
                        if 1 <= diff <= 4:
                            found[diff - 1] = eps
                    if not found:
                        continue
                    low, high = min(found), max(found)
                    for q in range(4):
                        value = turns[found[low]][(low - q) % 4]
                        if high > low:
                            value = jnp.where(group16 == low, value, turns[found[high]][(high - q) % 4])
                        start = pl.multiple_of((chunk * 4 + q) * GAP, 4)
                        lanes = slice(low * NO, (high + 1) * NO)
                        wide[e * 2 + half, pl.ds(start, NA), lanes] = value[:, lanes]
            return carry

        lax.fori_loop(0, 16, chunk_step, 0)

    def receive(slot):
        @pl.when(inside(SHIFTS[slot]))
        def _():
            halo_copy(3 - slot).wait_recv()

        @pl.when(jnp.logical_not(inside(SHIFTS[slot])))
        def _():
            halo[slot] = jnp.zeros(halo.shape[1:], BF16)

        place(SHIFTS[slot], lambda eps, lanes: halo[slot, eps, :, lanes])

    def gather(half):
        def gather_atom(atom, carry):
            for e in range(2):
                part = wide[e * 2 + half, pl.ds(atom, 2 * NO, stride=GAP), :]
                blocks[atom, e * 64 : (e + 1) * 64, half * 128 : (half + 1) * 128] = part.astype(BF16)
            return carry

        lax.fori_loop(0, NA, gather_atom, 0)

    loads[3].wait()
    place(0, lambda eps, lanes: own[eps, :, lanes])
    receive(0)
    receive(3)
    receive(1)
    gather(0)
    receive(2)
    gather(1)
    loads[4].wait()

    group = lane_group(NO)
    masks = [group == g for g in range(4)]

    def first_step(atom):
        stack = []
        for slot in range(NB):
            middle = jnp.dot(blocks[near[slot, atom]], kern[atom, slot], preferred_element_type=F32).astype(BF16)
            parts = [middle[g * NO : (g + 1) * NO, :] for g in range(4)]
            for i in range(3):
                value = None
                for g in range(4):
                    turn = (g - i) % 4
                    part = pltpu.roll(parts[g], NO * turn, 1) if turn else parts[g]
                    value = part if value is None else jnp.where(masks[g], part, value)
                stack.append(value)
        stack.append(jnp.zeros((NO, 128), BF16))
        return jnp.concatenate(stack, axis=0)

    def second_step(atom, stack):
        return jnp.dot(derivs[atom], stack, preferred_element_type=F32)

    def four_atoms(group):
        atoms = [4 * group + at for at in range(4)]
        stacks, results = [], []
        for at in range(4):
            stacks.append(first_step(atoms[at]))
            if at:
                results.append(second_step(atoms[at - 1], stacks[at - 1]))
        results.append(second_step(atoms[3], stacks[3]))
        return results

    def target(step):
        high = lax.rem(mom // 2 + 1 - step // 2, 2)
        low = lax.rem(mom + (step + 1) // 2, 2)
        return 2 * high + low

    def part_copy(step):
        return pltpu.make_async_remote_copy(
            src_ref=send_buf.at[step],
            dst_ref=recv_buf.at[step],
            send_sem=part_send.at[step],
            recv_sem=part_recv.at[step],
            device_id={"mom": target(step)},
            device_id_type=MESH,
        )

    def part_step(step, carry):
        for at, part in enumerate(four_atoms(target(step))):
            send_buf[step, at] = part.astype(BF16)
        part_copy(step).start()
        return carry

    lax.fori_loop(0, 3, part_step, 0)
    own_parts = four_atoms(mom)

    for step in range(3):
        part_copy(step).wait_recv()
    for at in range(4):
        total = own_parts[at]
        for step in range(3):
            total = total + recv_buf[step, at].astype(F32)
        for turn in range(4):
            turned[turn, at * 36 : at * 36 + NO, :] = pltpu.roll(total, NO * turn, 1) if turn else total
    for g in range(4):
        for high in range(8):
            value = None
            for low in range(4):
                line = turned[(low - g) % 4, pl.ds(high * 4 + low, 4, stride=36), :]
                value = line if value is None else jnp.where(masks[low][:4], line, value)
            start = (g % 2 * 8 + high) * 128
            out[g // 2, :, start : start + 128] = value

    for slot in range(4):
        @pl.when(inside(SHIFTS[slot]))
        def _():
            halo_copy(slot).wait_send()
    for step in range(3):
        part_copy(step).wait_send()


def body(green, coupling, gradient, neighbours, offsets):
    count, natoms = green.shape[1], green.shape[2]
    anywhere = pl.BlockSpec(memory_space=pl.ANY)
    vmem = pltpu.VMEM
    dma = pltpu.SemaphoreType.DMA
    return pl.pallas_call(
        kernel,
        out_shape=jax.ShapeDtypeStruct((count, natoms // 4, 2 * NO * NO), F32),
        in_specs=[anywhere] * 5,
        out_specs=pl.BlockSpec(memory_space=vmem),
        scratch_shapes=[
            vmem((2, NA, 2048), BF16),
            vmem((4, 2, NA, 2048), BF16),
            vmem((ROWS, 1024), BF16),
            vmem((NS * 9, NB, 1, NA), F32),
            pltpu.SMEM((NB, NA), jnp.int32),
            pltpu.SMEM((NW,), jnp.int32),
            vmem((NS * 9, 8, 128), F32),
            vmem((NO * STEP, 128), F32),
            vmem((NA, 24, 8, 128), F32),
            vmem((512, 128), F32),
            vmem((NA, NB, 256, 128), BF16),
            vmem((NA, NO, 512), BF16),
            vmem((4, 64 * GAP, 128), F32),
            vmem((NA, 128, 256), BF16),
            vmem((3, 4, NO, 128), BF16),
            vmem((3, 4, NO, 128), BF16),
            vmem((4, 4 * 36, 128), F32),
            dma((5,)),
            dma((4,)),
            dma((4,)),
            dma((3,)),
            dma((3,)),
        ],
        compiler_params=pltpu.CompilerParams(collective_id=0, has_side_effects=True),
    )(
        green[0],
        coupling.reshape(NS * 9, NB, 1, NA),
        gradient.reshape(ROWS, NO * NO),
        neighbours.T,
        offsets,
    )


def solution(mesh):
    in_specs = (P("mom", "energy", None, None), P("mom", None, None, None, None), P(), P(), P())
    out_specs = P("energy", "mom", None)
    return jax.shard_map(body, mesh=mesh, in_specs=in_specs, out_specs=out_specs, check_vma=False)
```

```python
import jax
import jax.numpy as jnp
from jax import lax
from jax.experimental import pallas as pl
from jax.experimental.pallas import tpu as pltpu
from jax.sharding import PartitionSpec as P

NO = 32
NB = 5
NW = 3
NA = 16
NS = 2 * NW
ROWS = NB * 3 * NA
STEP = 68
GAP = 20
MESH = pl.DeviceIdType.MESH
F32 = jnp.float32
BF16 = jnp.bfloat16
SHIFTS = (-2, -1, 1, 2)


def lane_group(rows, lanes=128):
    return lax.broadcasted_iota(jnp.int32, (rows, lanes), 1) // NO


def kernel(
    green, coupling, gradient, neighbours, offsets, out,
    own, halo, grad_v, coup_v, near, offs,
    coup_rows, spread, coef, flipped, kern, derivs, wide, blocks, send_buf, recv_buf, turned,
    local_sem, halo_send, halo_recv, part_send, part_recv,
):
    n_energy = lax.axis_size("energy")
    energy = lax.axis_index("energy")
    mom = lax.axis_index("mom")

    loads = [
        pltpu.make_async_copy(gradient, grad_v, local_sem.at[0]),
        pltpu.make_async_copy(coupling, coup_v, local_sem.at[1]),
        pltpu.make_async_copy(offsets, offs, local_sem.at[2]),
        pltpu.make_async_copy(green, own, local_sem.at[3]),
        pltpu.make_async_copy(neighbours, near, local_sem.at[4]),
    ]
    for load in loads:
        load.start()

    def inside(by):
        return jnp.logical_and(energy + by >= 0, energy + by < n_energy)

    barrier = pltpu.get_barrier_semaphore()
    for by in SHIFTS:
        @pl.when(inside(by))
        def _():
            pl.semaphore_signal(barrier, inc=1, device_id={"energy": energy + by}, device_id_type=MESH)
    for step in range(1, 4):
        pl.semaphore_signal(barrier, inc=1, device_id={"mom": lax.rem(mom + step, 4)}, device_id_type=MESH)
    expected = 3
    for by in SHIFTS:
        expected = expected + inside(by).astype(jnp.int32)

    pl.semaphore_wait(barrier, expected)

    def halo_copy(slot):
        by = SHIFTS[slot]
        return pltpu.make_async_remote_copy(
            src_ref=green,
            dst_ref=halo.at[3 - slot],
            send_sem=halo_send.at[slot],
            recv_sem=halo_recv.at[3 - slot],
            device_id={"energy": energy + by},
            device_id_type=MESH,
        )

    for slot in (0, 3, 1, 2):
        @pl.when(inside(SHIFTS[slot]))
        def _():
            halo_copy(slot).start()

    col = lax.broadcasted_iota(jnp.int32, (1, 512), 1)
    wanted = (col // NO) % 4 * 128 + col // 128 * NO + col % NO
    rows = lax.broadcasted_iota(jnp.int32, (512, 512), 0)
    pick = jnp.where(rows == wanted, 1.0, 0.0).astype(BF16)
    loads[0].wait()
    lines = []
    for chunk in range(8):
        tiles = []
        for g in range(4):
            parts = []
            for tile in range(4):
                block = 4 * tile + g
                if block < 3 * NB:
                    parts.append(grad_v[block * NA : (block + 1) * NA, chunk * 128 : (chunk + 1) * 128])
                else:
                    parts.append(jnp.zeros((NA, 128), BF16))
            tiles.append(jnp.concatenate(parts, axis=0))
        lines.append(jnp.concatenate(tiles, axis=1))
    packed = jnp.dot(jnp.concatenate(lines, axis=0), pick, preferred_element_type=F32)
    for chunk in range(8):
        for q in range(4):
            start = (chunk * 4 + q) * STEP
            spread[start : start + 64, :] = packed[chunk * 64 : (chunk + 1) * 64, q * 128 : (q + 1) * 128]

    loads[1].wait()
    loads[2].wait()

    for pair in range(NS * 9):
        for slot in range(NB):
            coup_rows[pair, slot : slot + 1, :NA] = coup_v[pair, slot]
    group8 = lane_group(8)
    weights = [
        [jnp.broadcast_to(jnp.where(offs[w] == size, 1.0, 0.0), (8, 128)) for w in range(NW)] for size in range(1, 5)
    ]

    def coef_step(j, carry):
        tables = [[coup_rows[s * 9 + 3 * i + j] for i in range(3)] for s in range(NS)]
        for atom in range(NA):
            terms = []
            for s in range(NS):
                first, second, third = [
                    jnp.broadcast_to(tables[s][i][:, atom : atom + 1], (8, 128)) for i in range(3)
                ]
                terms.append(jnp.where(group8 == 0, first, jnp.where(group8 == 1, second, third)))
            for size in range(1, 5):
                for g in range(2):
                    k = 4 * g + size - 1
                    total = None
                    for w in range(NW):
                        term = weights[size - 1][w] * terms[2 * w + g]
                        total = term if total is None else total + term
                    coef[atom, k * 3 + j] = total
        return carry

    lax.fori_loop(0, 3, coef_step, 0)

    def make_kernels(atom, carry):
        for tile in range(4):
            block = spread[pl.ds(tile * NA + atom, NO, stride=STEP), :]
            derivs[atom, :, tile * 128 : (tile + 1) * 128] = block.astype(BF16)
            flipped[tile * 128 : (tile + 1) * 128, :] = jnp.concatenate([block] * 4, axis=0).T
        for slot in range(NB):
            d = [flipped[(slot * 3 + j) * NO : (slot * 3 + j + 1) * NO, :] for j in range(3)]
            for k in range(8):
                total = None
                for j in range(3):
                    line = coef[atom, k * 3 + j, slot : slot + 1, :]
                    term = jnp.broadcast_to(line, (NO, 128)) * d[j]
                    total = term if total is None else total + term
                kern[atom, slot, k * NO : (k + 1) * NO, :] = total.astype(BF16)
        return carry

    lax.fori_loop(0, NA, make_kernels, 0)

    group16 = lane_group(NA)

    masks16 = [group16 == g for g in range(4)]

    def arrive(slot):
        @pl.when(inside(SHIFTS[slot]))
        def _():
            halo_copy(3 - slot).wait_recv()

        @pl.when(jnp.logical_not(inside(SHIFTS[slot])))
        def _():
            halo[slot] = jnp.zeros(halo.shape[1:], BF16)

    def place(half):
        def chunk_step(chunk, carry):
            lanes = pl.ds(pl.multiple_of(chunk * 128, 128), 128)
            turns = {}
            for e in range(2):
                for at in range(4):
                    row = e - (at + 1) * (1 - 2 * half)
                    if row not in turns:
                        block, eps = row // 2, row % 2
                        tile = own[eps, :, lanes] if block == 0 else halo[SHIFTS.index(block), eps, :, lanes]
                        tile = tile.astype(F32)
                        turns[row] = [tile] + [pltpu.roll(tile, NO * k, 1) for k in range(1, 4)]
            for e in range(2):
                for q in range(4):
                    value = None
                    for at in range(4):
                        part = turns[e - (at + 1) * (1 - 2 * half)][(at - q) % 4]
                        value = part if value is None else jnp.where(masks16[at], part, value)
                    start = pl.multiple_of((chunk * 4 + q) * GAP, 4)
                    wide[e * 2 + half, pl.ds(start, NA), :] = value
            return carry

        lax.fori_loop(0, 16, chunk_step, 0)

        def gather_atom(atom, carry):
            for e in range(2):
                part = wide[e * 2 + half, pl.ds(atom, 2 * NO, stride=GAP), :]
                blocks[atom, e * 64 : (e + 1) * 64, half * 128 : (half + 1) * 128] = part.astype(BF16)
            return carry

        lax.fori_loop(0, NA, gather_atom, 0)

    loads[3].wait()
    arrive(0)
    arrive(3)
    even = lax.rem(energy, 2) == 0

    @pl.when(even)
    def _():
        arrive(2)
        place(1)
        arrive(1)
        place(0)

    @pl.when(jnp.logical_not(even))
    def _():
        arrive(1)
        place(0)
        arrive(2)
        place(1)

    loads[4].wait()

    group = lane_group(NO)
    masks = [group == g for g in range(4)]

    def first_step(atom):
        stack = []
        for slot in range(NB):
            middle = jnp.dot(blocks[near[slot, atom]], kern[atom, slot], preferred_element_type=F32).astype(BF16)
            parts = [middle[g * NO : (g + 1) * NO, :] for g in range(4)]
            for i in range(3):
                value = None
                for g in range(4):
                    turn = (g - i) % 4
                    part = pltpu.roll(parts[g], NO * turn, 1) if turn else parts[g]
                    value = part if value is None else jnp.where(masks[g], part, value)
                stack.append(value)
        stack.append(jnp.zeros((NO, 128), BF16))
        return jnp.concatenate(stack, axis=0)

    def second_step(atom, stack):
        return jnp.dot(derivs[atom], stack, preferred_element_type=F32)

    def four_atoms(group):
        atoms = [4 * group + at for at in range(4)]
        stacks, results = [], []
        for at in range(4):
            stacks.append(first_step(atoms[at]))
            if at:
                results.append(second_step(atoms[at - 1], stacks[at - 1]))
        results.append(second_step(atoms[3], stacks[3]))
        return results

    def target(step):
        high = lax.rem(mom // 2 + 1 - step // 2, 2)
        low = lax.rem(mom + (step + 1) // 2, 2)
        return 2 * high + low

    def part_copy(step):
        return pltpu.make_async_remote_copy(
            src_ref=send_buf.at[step],
            dst_ref=recv_buf.at[step],
            send_sem=part_send.at[step],
            recv_sem=part_recv.at[step],
            device_id={"mom": target(step)},
            device_id_type=MESH,
        )

    def part_step(step, carry):
        for at, part in enumerate(four_atoms(target(step))):
            send_buf[step, at] = part.astype(BF16)
        part_copy(step).start()
        return carry

    lax.fori_loop(0, 3, part_step, 0)
    own_parts = four_atoms(mom)

    for step in range(3):
        part_copy(step).wait_recv()
    for at in range(4):
        total = own_parts[at]
        for step in range(3):
            total = total + recv_buf[step, at].astype(F32)
        for turn in range(4):
            turned[turn, at * 36 : at * 36 + NO, :] = pltpu.roll(total, NO * turn, 1) if turn else total
    for g in range(4):
        for high in range(8):
            value = None
            for low in range(4):
                line = turned[(low - g) % 4, pl.ds(high * 4 + low, 4, stride=36), :]
                value = line if value is None else jnp.where(masks[low][:4], line, value)
            start = (g % 2 * 8 + high) * 128
            out[g // 2, :, start : start + 128] = value

    for slot in range(4):
        @pl.when(inside(SHIFTS[slot]))
        def _():
            halo_copy(slot).wait_send()
    for step in range(3):
        part_copy(step).wait_send()


def body(green, coupling, gradient, neighbours, offsets):
    count, natoms = green.shape[1], green.shape[2]
    anywhere = pl.BlockSpec(memory_space=pl.ANY)
    vmem = pltpu.VMEM
    dma = pltpu.SemaphoreType.DMA
    return pl.pallas_call(
        kernel,
        out_shape=pltpu.VMEM((count, natoms // 4, 2 * NO * NO), F32),
        in_specs=[anywhere] * 5,
        out_specs=pl.BlockSpec(memory_space=vmem),
        scratch_shapes=[
            vmem((2, NA, 2048), BF16),
            vmem((4, 2, NA, 2048), BF16),
            vmem((ROWS, 1024), BF16),
            vmem((NS * 9, NB, 1, NA), F32),
            pltpu.SMEM((NB, NA), jnp.int32),
            pltpu.SMEM((NW,), jnp.int32),
            vmem((NS * 9, 8, 128), F32),
            vmem((NO * STEP, 128), F32),
            vmem((NA, 24, 8, 128), F32),
            vmem((512, 128), F32),
            vmem((NA, NB, 256, 128), BF16),
            vmem((NA, NO, 512), BF16),
            vmem((4, 64 * GAP, 128), F32),
            vmem((NA, 128, 256), BF16),
            vmem((3, 4, NO, 128), BF16),
            vmem((3, 4, NO, 128), BF16),
            vmem((4, 4 * 36, 128), F32),
            dma((5,)),
            dma((4,)),
            dma((4,)),
            dma((3,)),
            dma((3,)),
        ],
        compiler_params=pltpu.CompilerParams(collective_id=0, has_side_effects=True),
    )(
        green[0],
        coupling.reshape(NS * 9, NB, 1, NA),
        gradient.reshape(ROWS, NO * NO),
        neighbours.T,
        offsets,
    )


def solution(mesh):
    in_specs = (P("mom", "energy", None, None), P("mom", None, None, None, None), P(), P(), P())
    out_specs = P("energy", "mom", None)
    return jax.shard_map(body, mesh=mesh, in_specs=in_specs, out_specs=out_specs, check_vma=False)
```

```python
import jax
import jax.numpy as jnp
from jax import lax
from jax.experimental import pallas as pl
from jax.experimental.pallas import tpu as pltpu
from jax.sharding import PartitionSpec as P

NO = 32
NB = 5
NW = 3
NA = 16
NS = 2 * NW
ROWS = NB * 3 * NA
STEP = 68
GAP = 20
MESH = pl.DeviceIdType.MESH
F32 = jnp.float32
BF16 = jnp.bfloat16
SHIFTS = (-2, -1, 1, 2)


def lane_group(rows, lanes=128):
    return lax.broadcasted_iota(jnp.int32, (rows, lanes), 1) // NO


def kernel(
    green, coupling, gradient, neighbours, offsets, out,
    own, halo, grad_v, coup_v, near, offs,
    coup_rows, spread, coef, flipped, kern, derivs, wide, blocks, send_buf, recv_buf, turned,
    local_sem, halo_send, halo_recv, part_send, part_recv,
):
    n_energy = lax.axis_size("energy")
    energy = lax.axis_index("energy")
    mom = lax.axis_index("mom")

    loads = [
        pltpu.make_async_copy(gradient, grad_v, local_sem.at[0]),
        pltpu.make_async_copy(coupling, coup_v, local_sem.at[1]),
        pltpu.make_async_copy(offsets, offs, local_sem.at[2]),
        pltpu.make_async_copy(green, own, local_sem.at[3]),
        pltpu.make_async_copy(neighbours, near, local_sem.at[4]),
    ]
    for load in loads:
        load.start()

    def inside(by):
        return jnp.logical_and(energy + by >= 0, energy + by < n_energy)

    barrier = pltpu.get_barrier_semaphore()
    for by in SHIFTS:
        @pl.when(inside(by))
        def _():
            pl.semaphore_signal(barrier, inc=1, device_id={"energy": energy + by}, device_id_type=MESH)
    for step in range(1, 4):
        pl.semaphore_signal(barrier, inc=1, device_id={"mom": lax.rem(mom + step, 4)}, device_id_type=MESH)
    expected = 3
    for by in SHIFTS:
        expected = expected + inside(by).astype(jnp.int32)

    pl.semaphore_wait(barrier, expected)

    def halo_copy(slot):
        by = SHIFTS[slot]
        return pltpu.make_async_remote_copy(
            src_ref=green,
            dst_ref=halo.at[3 - slot],
            send_sem=halo_send.at[slot],
            recv_sem=halo_recv.at[3 - slot],
            device_id={"energy": energy + by},
            device_id_type=MESH,
        )

    for slot in (0, 3, 1, 2):
        @pl.when(inside(SHIFTS[slot]))
        def _():
            halo_copy(slot).start()

    col = lax.broadcasted_iota(jnp.int32, (1, 512), 1)
    wanted = (col // NO) % 4 * 128 + col // 128 * NO + col % NO
    rows = lax.broadcasted_iota(jnp.int32, (512, 512), 0)
    pick = jnp.where(rows == wanted, 1.0, 0.0).astype(BF16)
    loads[0].wait()
    lines = []
    for chunk in range(8):
        tiles = []
        for g in range(4):
            parts = []
            for tile in range(4):
                block = 4 * tile + g
                if block < 3 * NB:
                    parts.append(grad_v[block * NA : (block + 1) * NA, chunk * 128 : (chunk + 1) * 128])
                else:
                    parts.append(jnp.zeros((NA, 128), BF16))
            tiles.append(jnp.concatenate(parts, axis=0))
        lines.append(jnp.concatenate(tiles, axis=1))
    packed = jnp.dot(jnp.concatenate(lines, axis=0), pick, preferred_element_type=F32)
    for chunk in range(8):
        for q in range(4):
            start = (chunk * 4 + q) * STEP
            spread[start : start + 64, :] = packed[chunk * 64 : (chunk + 1) * 64, q * 128 : (q + 1) * 128]

    loads[1].wait()
    loads[2].wait()

    for pair in range(NS * 9):
        for slot in range(NB):
            coup_rows[pair, slot : slot + 1, :NA] = coup_v[pair, slot]
    group8 = lane_group(8)
    weights = [
        [jnp.broadcast_to(jnp.where(offs[w] == size, 1.0, 0.0), (8, 128)) for w in range(NW)] for size in range(1, 5)
    ]

    def coef_step(j, carry):
        tables = [[coup_rows[s * 9 + 3 * i + j] for i in range(3)] for s in range(NS)]
        for atom in range(NA):
            terms = []
            for s in range(NS):
                first, second, third = [
                    jnp.broadcast_to(tables[s][i][:, atom : atom + 1], (8, 128)) for i in range(3)
                ]
                terms.append(jnp.where(group8 == 0, first, jnp.where(group8 == 1, second, third)))
            for size in range(1, 5):
                for g in range(2):
                    k = 4 * g + size - 1
                    total = None
                    for w in range(NW):
                        term = weights[size - 1][w] * terms[2 * w + g]
                        total = term if total is None else total + term
                    coef[atom, k * 3 + j] = total
        return carry

    lax.fori_loop(0, 3, coef_step, 0)

    def make_kernels(atom, carry):
        for tile in range(4):
            block = spread[pl.ds(tile * NA + atom, NO, stride=STEP), :]
            derivs[atom, :, tile * 128 : (tile + 1) * 128] = block.astype(BF16)
            flipped[tile * 128 : (tile + 1) * 128, :] = jnp.concatenate([block] * 4, axis=0).T
        for slot in range(NB):
            d = [flipped[(slot * 3 + j) * NO : (slot * 3 + j + 1) * NO, :] for j in range(3)]
            for k in range(8):
                total = None
                for j in range(3):
                    line = coef[atom, k * 3 + j, slot : slot + 1, :]
                    term = jnp.broadcast_to(line, (NO, 128)) * d[j]
                    total = term if total is None else total + term
                kern[atom, slot, k * NO : (k + 1) * NO, :] = total.astype(BF16)
        return carry

    lax.fori_loop(0, NA, make_kernels, 0)

    group16 = lane_group(NA)

    masks16 = [group16 == g for g in range(4)]

    def arrive(slot):
        @pl.when(inside(SHIFTS[slot]))
        def _():
            halo_copy(3 - slot).wait_recv()

        @pl.when(jnp.logical_not(inside(SHIFTS[slot])))
        def _():
            halo[slot] = jnp.zeros(halo.shape[1:], BF16)

    def place(half):
        def chunk_step(chunk, carry):
            lanes = pl.ds(pl.multiple_of(chunk * 128, 128), 128)
            turns = {}
            for e in range(2):
                for at in range(4):
                    row = e - (at + 1) * (1 - 2 * half)
                    if row not in turns:
                        block, eps = row // 2, row % 2
                        tile = own[eps, :, lanes] if block == 0 else halo[SHIFTS.index(block), eps, :, lanes]
                        turns[row] = [tile] + [pltpu.roll(tile, NO * k, 1) for k in range(1, 4)]
            for e in range(2):
                for q in range(4):
                    value = None
                    for at in range(4):
                        part = turns[e - (at + 1) * (1 - 2 * half)][(at - q) % 4]
                        value = part if value is None else jnp.where(masks16[at], part, value)
                    start = pl.multiple_of((chunk * 4 + q) * GAP, 4)
                    wide[e * 2 + half, pl.ds(start, NA), :] = value.astype(F32)
            return carry

        lax.fori_loop(0, 16, chunk_step, 0, unroll=4)

        def gather_atom(atom, carry):
            for e in range(2):
                part = wide[e * 2 + half, pl.ds(atom, 2 * NO, stride=GAP), :]
                blocks[atom, e * 64 : (e + 1) * 64, half * 128 : (half + 1) * 128] = part.astype(BF16)
            return carry

        lax.fori_loop(0, NA, gather_atom, 0, unroll=4)

    loads[3].wait()
    arrive(0)
    arrive(3)
    even = lax.rem(energy, 2) == 0

    @pl.when(even)
    def _():
        arrive(2)
        place(1)
        arrive(1)
        place(0)

    @pl.when(jnp.logical_not(even))
    def _():
        arrive(1)
        place(0)
        arrive(2)
        place(1)

    loads[4].wait()

    group = lane_group(NO)
    masks = [group == g for g in range(4)]

    def first_step(atom):
        stack = []
        for slot in range(NB):
            middle = jnp.dot(blocks[near[slot, atom]], kern[atom, slot], preferred_element_type=F32).astype(BF16)
            parts = [middle[g * NO : (g + 1) * NO, :] for g in range(4)]
            for i in range(3):
                value = None
                for g in range(4):
                    turn = (g - i) % 4
                    part = pltpu.roll(parts[g], NO * turn, 1) if turn else parts[g]
                    value = part if value is None else jnp.where(masks[g], part, value)
                stack.append(value)
        stack.append(jnp.zeros((NO, 128), BF16))
        return jnp.concatenate(stack, axis=0)

    def second_step(atom, stack):
        return jnp.dot(derivs[atom], stack, preferred_element_type=F32)

    def four_atoms(group):
        atoms = [4 * group + at for at in range(4)]
        stacks, results = [], []
        for at in range(4):
            stacks.append(first_step(atoms[at]))
            if at:
                results.append(second_step(atoms[at - 1], stacks[at - 1]))
        results.append(second_step(atoms[3], stacks[3]))
        return results

    def target(step):
        high = lax.rem(mom // 2 + 1 - step // 2, 2)
        low = lax.rem(mom + (step + 1) // 2, 2)
        return 2 * high + low

    def part_copy(step):
        return pltpu.make_async_remote_copy(
            src_ref=send_buf.at[step],
            dst_ref=recv_buf.at[step],
            send_sem=part_send.at[step],
            recv_sem=part_recv.at[step],
            device_id={"mom": target(step)},
            device_id_type=MESH,
        )

    def part_step(step, carry):
        for at, part in enumerate(four_atoms(target(step))):
            send_buf[step, at] = part.astype(BF16)
        part_copy(step).start()
        return carry

    lax.fori_loop(0, 3, part_step, 0)
    own_parts = four_atoms(mom)

    for step in range(3):
        part_copy(step).wait_recv()
    for at in range(4):
        total = own_parts[at]
        for step in range(3):
            total = total + recv_buf[step, at].astype(F32)
        for turn in range(4):
            turned[turn, at * 36 : at * 36 + NO, :] = pltpu.roll(total, NO * turn, 1) if turn else total
    for g in range(4):
        for high in range(8):
            value = None
            for low in range(4):
                line = turned[(low - g) % 4, pl.ds(high * 4 + low, 4, stride=36), :]
                value = line if value is None else jnp.where(masks[low][:4], line, value)
            start = (g % 2 * 8 + high) * 128
            out[g // 2, :, start : start + 128] = value

    for slot in range(4):
        @pl.when(inside(SHIFTS[slot]))
        def _():
            halo_copy(slot).wait_send()
    for step in range(3):
        part_copy(step).wait_send()


def body(green, coupling, gradient, neighbours, offsets):
    count, natoms = green.shape[1], green.shape[2]
    anywhere = pl.BlockSpec(memory_space=pl.ANY)
    vmem = pltpu.VMEM
    dma = pltpu.SemaphoreType.DMA
    return pl.pallas_call(
        kernel,
        out_shape=pltpu.VMEM((count, natoms // 4, 2 * NO * NO), F32),
        in_specs=[anywhere] * 5,
        out_specs=pl.BlockSpec(memory_space=vmem),
        scratch_shapes=[
            vmem((2, NA, 2048), BF16),
            vmem((4, 2, NA, 2048), BF16),
            vmem((ROWS, 1024), BF16),
            vmem((NS * 9, NB, 1, NA), F32),
            pltpu.SMEM((NB, NA), jnp.int32),
            pltpu.SMEM((NW,), jnp.int32),
            vmem((NS * 9, 8, 128), F32),
            vmem((NO * STEP, 128), F32),
            vmem((NA, 24, 8, 128), F32),
            vmem((512, 128), F32),
            vmem((NA, NB, 256, 128), BF16),
            vmem((NA, NO, 512), BF16),
            vmem((4, 64 * GAP, 128), F32),
            vmem((NA, 128, 256), BF16),
            vmem((3, 4, NO, 128), BF16),
            vmem((3, 4, NO, 128), BF16),
            vmem((4, 4 * 36, 128), F32),
            dma((5,)),
            dma((4,)),
            dma((4,)),
            dma((3,)),
            dma((3,)),
        ],
        compiler_params=pltpu.CompilerParams(collective_id=0, has_side_effects=True),
    )(
        green[0],
        coupling.reshape(NS * 9, NB, 1, NA),
        gradient.reshape(ROWS, NO * NO),
        neighbours.T,
        offsets,
    )


def solution(mesh):
    in_specs = (P("mom", "energy", None, None), P("mom", None, None, None, None), P(), P(), P())
    out_specs = P("energy", "mom", None)
    return jax.shard_map(body, mesh=mesh, in_specs=in_specs, out_specs=out_specs, check_vma=False)
```

```python
import jax
import jax.numpy as jnp
from jax import lax
from jax.experimental import pallas as pl
from jax.experimental.pallas import tpu as pltpu
from jax.sharding import PartitionSpec as P

NO = 32
NB = 5
NW = 3
NA = 16
NS = 2 * NW
ROWS = NB * 3 * NA
STEP = 68
GAP = 20
MESH = pl.DeviceIdType.MESH
F32 = jnp.float32
BF16 = jnp.bfloat16
SHIFTS = (-2, -1, 1, 2)


def lane_group(rows, lanes=128):
    return lax.broadcasted_iota(jnp.int32, (rows, lanes), 1) // NO


def kernel(
    green, coupling, gradient, neighbours, offsets, out,
    own, halo, grad_v, coup_v, near, offs,
    coup_rows, spread, coef, flipped, kern, derivs, wide, blocks, send_buf, recv_buf, turned,
    local_sem, halo_send, halo_recv, part_send, part_recv,
):
    n_energy = lax.axis_size("energy")
    energy = lax.axis_index("energy")
    mom = lax.axis_index("mom")

    loads = [
        pltpu.make_async_copy(gradient, grad_v, local_sem.at[0]),
        pltpu.make_async_copy(coupling, coup_v, local_sem.at[1]),
        pltpu.make_async_copy(offsets, offs, local_sem.at[2]),
        pltpu.make_async_copy(green, own, local_sem.at[3]),
        pltpu.make_async_copy(neighbours, near, local_sem.at[4]),
    ]
    for load in loads:
        load.start()

    def inside(by):
        return jnp.logical_and(energy + by >= 0, energy + by < n_energy)

    barrier = pltpu.get_barrier_semaphore()
    for by in SHIFTS:
        @pl.when(inside(by))
        def _():
            pl.semaphore_signal(barrier, inc=1, device_id={"energy": energy + by}, device_id_type=MESH)
    for step in range(1, 4):
        pl.semaphore_signal(barrier, inc=1, device_id={"mom": lax.rem(mom + step, 4)}, device_id_type=MESH)
    expected = 3
    for by in SHIFTS:
        expected = expected + inside(by).astype(jnp.int32)

    pl.semaphore_wait(barrier, expected)

    def halo_copy(slot):
        by = SHIFTS[slot]
        return pltpu.make_async_remote_copy(
            src_ref=green,
            dst_ref=halo.at[3 - slot],
            send_sem=halo_send.at[slot],
            recv_sem=halo_recv.at[3 - slot],
            device_id={"energy": energy + by},
            device_id_type=MESH,
        )

    for slot in (0, 3, 1, 2):
        @pl.when(inside(SHIFTS[slot]))
        def _():
            halo_copy(slot).start()

    col = lax.broadcasted_iota(jnp.int32, (1, 512), 1)
    wanted = (col // NO) % 4 * 128 + col // 128 * NO + col % NO
    rows = lax.broadcasted_iota(jnp.int32, (512, 512), 0)
    pick = jnp.where(rows == wanted, 1.0, 0.0).astype(BF16)
    loads[0].wait()
    lines = []
    for chunk in range(8):
        tiles = []
        for g in range(4):
            parts = []
            for tile in range(4):
                block = 4 * tile + g
                if block < 3 * NB:
                    parts.append(grad_v[block * NA : (block + 1) * NA, chunk * 128 : (chunk + 1) * 128])
                else:
                    parts.append(jnp.zeros((NA, 128), BF16))
            tiles.append(jnp.concatenate(parts, axis=0))
        lines.append(jnp.concatenate(tiles, axis=1))
    packed = jnp.dot(jnp.concatenate(lines, axis=0), pick, preferred_element_type=F32)
    for chunk in range(8):
        for q in range(4):
            start = (chunk * 4 + q) * STEP
            spread[start : start + 64, :] = packed[chunk * 64 : (chunk + 1) * 64, q * 128 : (q + 1) * 128]

    loads[1].wait()
    loads[2].wait()

    for pair in range(NS * 9):
        for slot in range(NB):
            coup_rows[pair, slot : slot + 1, :NA] = coup_v[pair, slot]
    group8 = lane_group(8)
    weights = [
        [jnp.broadcast_to(jnp.where(offs[w] == size, 1.0, 0.0), (8, 128)) for w in range(NW)] for size in range(1, 5)
    ]

    def coef_step(j, carry):
        tables = [[coup_rows[s * 9 + 3 * i + j] for i in range(3)] for s in range(NS)]
        for atom in range(NA):
            terms = []
            for s in range(NS):
                first, second, third = [
                    jnp.broadcast_to(tables[s][i][:, atom : atom + 1], (8, 128)) for i in range(3)
                ]
                terms.append(jnp.where(group8 == 0, first, jnp.where(group8 == 1, second, third)))
            for size in range(1, 5):
                for g in range(2):
                    k = 4 * g + size - 1
                    total = None
                    for w in range(NW):
                        term = weights[size - 1][w] * terms[2 * w + g]
                        total = term if total is None else total + term
                    coef[atom, k * 3 + j] = total
        return carry

    lax.fori_loop(0, 3, coef_step, 0)

    def make_kernels(atom, carry):
        for tile in range(4):
            block = spread[pl.ds(tile * NA + atom, NO, stride=STEP), :]
            derivs[atom, :, tile * 128 : (tile + 1) * 128] = block.astype(BF16)
            flipped[tile * 128 : (tile + 1) * 128, :] = jnp.concatenate([block] * 4, axis=0).T
        for slot in range(NB):
            d = [flipped[(slot * 3 + j) * NO : (slot * 3 + j + 1) * NO, :] for j in range(3)]
            for k in range(8):
                total = None
                for j in range(3):
                    line = coef[atom, k * 3 + j, slot : slot + 1, :]
                    term = jnp.broadcast_to(line, (NO, 128)) * d[j]
                    total = term if total is None else total + term
                kern[atom, slot, k * NO : (k + 1) * NO, :] = total.astype(BF16)
        return carry

    lax.fori_loop(0, NA, make_kernels, 0)

    group16 = lane_group(NA)

    masks16 = [group16 == g for g in range(4)]

    def arrive(slot):
        @pl.when(inside(SHIFTS[slot]))
        def _():
            halo_copy(3 - slot).wait_recv()

        @pl.when(jnp.logical_not(inside(SHIFTS[slot])))
        def _():
            halo[slot] = jnp.zeros(halo.shape[1:], BF16)

    def place(half):
        def chunk_step(chunk, carry):
            lanes = pl.ds(pl.multiple_of(chunk * 128, 128), 128)
            turns = {}
            for e in range(2):
                for at in range(4):
                    row = e - (at + 1) * (1 - 2 * half)
                    if row not in turns:
                        block, eps = row // 2, row % 2
                        tile = own[eps, :, lanes] if block == 0 else halo[SHIFTS.index(block), eps, :, lanes]
                        turns[row] = [tile] + [pltpu.roll(tile, NO * k, 1) for k in range(1, 4)]
            for e in range(2):
                for q in range(4):
                    value = None
                    for at in range(4):
                        part = turns[e - (at + 1) * (1 - 2 * half)][(at - q) % 4]
                        value = part if value is None else jnp.where(masks16[at], part, value)
                    start = pl.multiple_of((chunk * 4 + q) * GAP, 4)
                    wide[e * 2 + half, pl.ds(start, NA), :] = value.astype(F32)
            return carry

        lax.fori_loop(0, 16, chunk_step, 0, unroll=4)

        def gather_atom(atom, carry):
            for e in range(2):
                part = wide[e * 2 + half, pl.ds(atom, 2 * NO, stride=GAP), :]
                blocks[atom, e * 64 : (e + 1) * 64, half * 128 : (half + 1) * 128] = part.astype(BF16)
            return carry

        lax.fori_loop(0, NA, gather_atom, 0, unroll=4)

    loads[3].wait()
    arrive(0)
    arrive(3)
    even = lax.rem(energy, 2) == 0

    @pl.when(even)
    def _():
        arrive(2)
        place(1)
        arrive(1)
        place(0)

    @pl.when(jnp.logical_not(even))
    def _():
        arrive(1)
        place(0)
        arrive(2)
        place(1)

    loads[4].wait()

    group = lane_group(NO)
    masks = [group == g for g in range(4)]

    def first_step(atom):
        stack = []
        for slot in range(NB):
            middle = jnp.dot(blocks[near[slot, atom]], kern[atom, slot], preferred_element_type=F32).astype(BF16)
            parts = [middle[g * NO : (g + 1) * NO, :] for g in range(4)]
            for i in range(3):
                value = None
                for g in range(4):
                    turn = (g - i) % 4
                    part = pltpu.roll(parts[g], NO * turn, 1) if turn else parts[g]
                    value = part if value is None else jnp.where(masks[g], part, value)
                stack.append(value)
        stack.append(jnp.zeros((NO, 128), BF16))
        return jnp.concatenate(stack, axis=0)

    def second_step(atom, stack):
        return jnp.dot(derivs[atom], stack, preferred_element_type=F32)

    def target(step):
        high = lax.rem(mom // 2 + 1 - step // 2, 2)
        low = lax.rem(mom + (step + 1) // 2, 2)
        return 2 * high + low

    def part_copy(step):
        return pltpu.make_async_remote_copy(
            src_ref=send_buf.at[step],
            dst_ref=recv_buf.at[step],
            send_sem=part_send.at[step],
            recv_sem=part_recv.at[step],
            device_id={"mom": target(step)},
            device_id_type=MESH,
        )

    own_parts = []

    def finish(step, at, atom, stack):
        part = second_step(atom, stack)
        if step == 3:
            own_parts.append(part)
            return
        send_buf[step, at] = part.astype(BF16)
        if at == 3:
            part_copy(step).start()

    waiting = None
    for step in range(4):
        for at in range(4):
            atom = 4 * target(step) + at
            stack = first_step(atom)
            if waiting is not None:
                finish(*waiting)
            waiting = (step, at, atom, stack)
    finish(*waiting)

    for step in range(3):
        part_copy(step).wait_recv()
    for at in range(4):
        total = own_parts[at]
        for step in range(3):
            total = total + recv_buf[step, at].astype(F32)
        for turn in range(4):
            turned[turn, at * 36 : at * 36 + NO, :] = pltpu.roll(total, NO * turn, 1) if turn else total
    for g in range(4):
        for high in range(8):
            value = None
            for low in range(4):
                line = turned[(low - g) % 4, pl.ds(high * 4 + low, 4, stride=36), :]
                value = line if value is None else jnp.where(masks[low][:4], line, value)
            start = (g % 2 * 8 + high) * 128
            out[g // 2, :, start : start + 128] = value

    for slot in range(4):
        @pl.when(inside(SHIFTS[slot]))
        def _():
            halo_copy(slot).wait_send()
    for step in range(3):
        part_copy(step).wait_send()


def body(green, coupling, gradient, neighbours, offsets):
    count, natoms = green.shape[1], green.shape[2]
    anywhere = pl.BlockSpec(memory_space=pl.ANY)
    vmem = pltpu.VMEM
    dma = pltpu.SemaphoreType.DMA
    return pl.pallas_call(
        kernel,
        out_shape=pltpu.VMEM((count, natoms // 4, 2 * NO * NO), F32),
        in_specs=[anywhere] * 5,
        out_specs=pl.BlockSpec(memory_space=vmem),
        scratch_shapes=[
            vmem((2, NA, 2048), BF16),
            vmem((4, 2, NA, 2048), BF16),
            vmem((ROWS, 1024), BF16),
            vmem((NS * 9, NB, 1, NA), F32),
            pltpu.SMEM((NB, NA), jnp.int32),
            pltpu.SMEM((NW,), jnp.int32),
            vmem((NS * 9, 8, 128), F32),
            vmem((NO * STEP, 128), F32),
            vmem((NA, 24, 8, 128), F32),
            vmem((512, 128), F32),
            vmem((NA, NB, 256, 128), BF16),
            vmem((NA, NO, 512), BF16),
            vmem((4, 64 * GAP, 128), F32),
            vmem((NA, 128, 256), BF16),
            vmem((3, 4, NO, 128), BF16),
            vmem((3, 4, NO, 128), BF16),
            vmem((4, 4 * 36, 128), F32),
            dma((5,)),
            dma((4,)),
            dma((4,)),
            dma((3,)),
            dma((3,)),
        ],
        compiler_params=pltpu.CompilerParams(collective_id=0, has_side_effects=True),
    )(
        green[0],
        coupling.reshape(NS * 9, NB, 1, NA),
        gradient.reshape(ROWS, NO * NO),
        neighbours.T,
        offsets,
    )


def solution(mesh):
    in_specs = (P("mom", "energy", None, None), P("mom", None, None, None, None), P(), P(), P())
    out_specs = P("energy", "mom", None)
    return jax.shard_map(body, mesh=mesh, in_specs=in_specs, out_specs=out_specs, check_vma=False)
```

```python
import jax
import jax.numpy as jnp
from jax import lax
from jax.experimental import pallas as pl
from jax.experimental.pallas import tpu as pltpu
from jax.sharding import PartitionSpec as P

NO = 32
NB = 5
NW = 3
NA = 16
NS = 2 * NW
ROWS = NB * 3 * NA
STEP = 68
GAP = 20
STOPS = (0, 0, 2, 3)
MESH = pl.DeviceIdType.MESH
F32 = jnp.float32
BF16 = jnp.bfloat16
SHIFTS = (-2, -1, 1, 2)


def lane_group(rows, lanes=128):
    return lax.broadcasted_iota(jnp.int32, (rows, lanes), 1) // NO


def kernel(
    green, coupling, gradient, neighbours, offsets, out,
    own, halo, grad_v, coup_v, near, offs,
    coup_rows, spread, coef, flipped, kern, derivs, wide, blocks, send_buf, recv_buf, turned,
    local_sem, halo_send, halo_recv, part_send, part_recv,
):
    n_energy = lax.axis_size("energy")
    energy = lax.axis_index("energy")
    mom = lax.axis_index("mom")

    loads = [
        pltpu.make_async_copy(gradient, grad_v, local_sem.at[0]),
        pltpu.make_async_copy(coupling, coup_v, local_sem.at[1]),
        pltpu.make_async_copy(offsets, offs, local_sem.at[2]),
        pltpu.make_async_copy(green, own, local_sem.at[3]),
        pltpu.make_async_copy(neighbours, near, local_sem.at[4]),
    ]
    for load in loads:
        load.start()

    def inside(by):
        return jnp.logical_and(energy + by >= 0, energy + by < n_energy)

    barrier = pltpu.get_barrier_semaphore()
    odd = lax.rem(energy, 2)
    mate = energy + 1 - 2 * odd
    for by in (-2, 2):
        @pl.when(inside(by))
        def _():
            pl.semaphore_signal(barrier, inc=1, device_id={"energy": energy + by}, device_id_type=MESH)
    pl.semaphore_signal(barrier, inc=1, device_id={"energy": mate}, device_id_type=MESH)
    for step in range(1, 4):
        pl.semaphore_signal(barrier, inc=1, device_id={"mom": lax.rem(mom + step, 4)}, device_id_type=MESH)
    expected = 4
    for by in (-2, 2):
        expected = expected + inside(by).astype(jnp.int32)

    pl.semaphore_wait(barrier, expected)

    def halo_copy(source, eps, slot, kind, peer):
        return pltpu.make_async_remote_copy(
            src_ref=source.at[eps // 2, :, eps % 2 * 1024 : eps % 2 * 1024 + 1024],
            dst_ref=halo.at[slot, eps // 2, :, eps % 2 * 1024 : eps % 2 * 1024 + 1024],
            send_sem=halo_send.at[kind, eps],
            recv_sem=halo_recv.at[slot, eps],
            device_id={"energy": peer},
            device_id_type=MESH,
        )

    def up(eps):
        return halo_copy(green, eps, 0, 0, energy + 2)

    def down(eps):
        return halo_copy(green, eps, 3, 1, energy - 2)

    def across_pair(eps):
        return halo_copy(green, eps, 1 + odd, 2, mate)

    def forward(eps):
        return halo_copy(halo.at[3 - 3 * odd], eps, 2 - odd, 3, mate)

    def arrived(slot, eps):
        halo_copy(green, eps, slot, 0, mate).wait_recv()

    passing = jnp.logical_or(jnp.logical_and(odd == 0, inside(2)), jnp.logical_and(odd == 1, inside(-2)))
    for eps in range(4):
        @pl.when(inside(-2))
        def _():
            down(eps).start()

        @pl.when(inside(2))
        def _():
            up(eps).start()

        across_pair(eps).start()
    for slot in range(4):
        @pl.when(jnp.logical_not(inside(SHIFTS[slot])))
        def _():
            halo[slot] = jnp.zeros(halo.shape[1:], BF16)

    col = lax.broadcasted_iota(jnp.int32, (1, 512), 1)
    wanted = (col // NO) % 4 * 128 + col // 128 * NO + col % NO
    rows = lax.broadcasted_iota(jnp.int32, (512, 512), 0)
    pick = jnp.where(rows == wanted, 1.0, 0.0).astype(BF16)
    loads[0].wait()
    lines = []
    for chunk in range(8):
        tiles = []
        for g in range(4):
            parts = []
            for tile in range(4):
                block = 4 * tile + g
                if block < 3 * NB:
                    parts.append(grad_v[block * NA : (block + 1) * NA, chunk * 128 : (chunk + 1) * 128])
                else:
                    parts.append(jnp.zeros((NA, 128), BF16))
            tiles.append(jnp.concatenate(parts, axis=0))
        lines.append(jnp.concatenate(tiles, axis=1))
    packed = jnp.dot(jnp.concatenate(lines, axis=0), pick, preferred_element_type=F32)
    for chunk in range(8):
        for q in range(4):
            start = (chunk * 4 + q) * STEP
            spread[start : start + 64, :] = packed[chunk * 64 : (chunk + 1) * 64, q * 128 : (q + 1) * 128]

    loads[1].wait()
    loads[2].wait()

    for pair in range(NS * 9):
        for slot in range(NB):
            coup_rows[pair, slot : slot + 1, :NA] = coup_v[pair, slot]
    group8 = lane_group(8)
    weights = [
        [jnp.broadcast_to(jnp.where(offs[w] == size, 1.0, 0.0), (8, 128)) for w in range(NW)] for size in range(1, 5)
    ]

    def coef_step(j, carry):
        tables = [[coup_rows[s * 9 + 3 * i + j] for i in range(3)] for s in range(NS)]
        for atom in range(NA):
            terms = []
            for s in range(NS):
                first, second, third = [
                    jnp.broadcast_to(tables[s][i][:, atom : atom + 1], (8, 128)) for i in range(3)
                ]
                terms.append(jnp.where(group8 == 0, first, jnp.where(group8 == 1, second, third)))
            for size in range(1, 5):
                for g in range(2):
                    k = 4 * g + size - 1
                    total = None
                    for w in range(NW):
                        term = weights[size - 1][w] * terms[2 * w + g]
                        total = term if total is None else total + term
                    coef[atom, k * 3 + j] = total
        return carry

    lax.fori_loop(0, 3, coef_step, 0)

    def make_kernels(atom, carry):
        for tile in range(4):
            block = spread[pl.ds(tile * NA + atom, NO, stride=STEP), :]
            derivs[atom, :, tile * 128 : (tile + 1) * 128] = block.astype(BF16)
            flipped[tile * 128 : (tile + 1) * 128, :] = jnp.concatenate([block] * 4, axis=0).T
        for slot in range(NB):
            d = [flipped[(slot * 3 + j) * NO : (slot * 3 + j + 1) * NO, :] for j in range(3)]
            for k in range(8):
                total = None
                for j in range(3):
                    line = coef[atom, k * 3 + j, slot : slot + 1, :]
                    term = jnp.broadcast_to(line, (NO, 128)) * d[j]
                    total = term if total is None else total + term
                kern[atom, slot, k * NO : (k + 1) * NO, :] = total.astype(BF16)
        return carry

    def pass_on(eps):
        @pl.when(passing)
        def _():
            arrived(3 - 3 * odd, eps)
            forward(eps).start()

    done = 0
    for eps, stop in enumerate(STOPS):
        if stop > done:
            lax.fori_loop(done, stop, make_kernels, 0)
        done = stop
        pass_on(eps)
    lax.fori_loop(done, NA, make_kernels, 0)

    group16 = lane_group(NA)

    masks16 = [group16 == g for g in range(4)]

    def arrive(slot):
        @pl.when(inside(SHIFTS[slot]))
        def _():
            for eps in range(4):
                arrived(slot, eps)

    def place(half):
        def chunk_step(chunk, carry):
            lanes = pl.ds(pl.multiple_of(chunk * 128, 128), 128)
            turns = {}
            for e in range(2):
                for at in range(4):
                    row = e - (at + 1) * (1 - 2 * half)
                    if row not in turns:
                        block, eps = row // 2, row % 2
                        tile = own[eps, :, lanes] if block == 0 else halo[SHIFTS.index(block), eps, :, lanes]
                        turns[row] = [tile] + [pltpu.roll(tile, NO * k, 1) for k in range(1, 4)]
            for e in range(2):
                for q in range(4):
                    value = None
                    for at in range(4):
                        part = turns[e - (at + 1) * (1 - 2 * half)][(at - q) % 4]
                        value = part if value is None else jnp.where(masks16[at], part, value)
                    start = pl.multiple_of((chunk * 4 + q) * GAP, 4)
                    wide[e * 2 + half, pl.ds(start, NA), :] = value.astype(F32)
            return carry

        lax.fori_loop(0, 16, chunk_step, 0, unroll=4)

        def gather_atom(atom, carry):
            for e in range(2):
                part = wide[e * 2 + half, pl.ds(atom, 2 * NO, stride=GAP), :]
                blocks[atom, e * 64 : (e + 1) * 64, half * 128 : (half + 1) * 128] = part.astype(BF16)
            return carry

        lax.fori_loop(0, NA, gather_atom, 0, unroll=4)

    loads[3].wait()
    @pl.when(odd == 0)
    def _():
        arrive(2)
        place(1)
        arrive(0)
        arrive(1)
        place(0)

    @pl.when(odd == 1)
    def _():
        arrive(1)
        place(0)
        arrive(3)
        arrive(2)
        place(1)

    loads[4].wait()

    group = lane_group(NO)
    masks = [group == g for g in range(4)]

    def first_step(atom):
        stack = []
        for slot in range(NB):
            middle = jnp.dot(blocks[near[slot, atom]], kern[atom, slot], preferred_element_type=F32).astype(BF16)
            parts = [middle[g * NO : (g + 1) * NO, :] for g in range(4)]
            for i in range(3):
                value = None
                for g in range(4):
                    turn = (g - i) % 4
                    part = pltpu.roll(parts[g], NO * turn, 1) if turn else parts[g]
                    value = part if value is None else jnp.where(masks[g], part, value)
                stack.append(value)
        stack.append(jnp.zeros((NO, 128), BF16))
        return jnp.concatenate(stack, axis=0)

    def second_step(atom, stack):
        return jnp.dot(derivs[atom], stack, preferred_element_type=F32)

    def target(step):
        high = lax.rem(mom // 2 + 1 - step // 2, 2)
        low = lax.rem(mom + (step + 1) // 2, 2)
        return 2 * high + low

    def part_copy(step):
        return pltpu.make_async_remote_copy(
            src_ref=send_buf.at[step],
            dst_ref=recv_buf.at[step],
            send_sem=part_send.at[step],
            recv_sem=part_recv.at[step],
            device_id={"mom": target(step)},
            device_id_type=MESH,
        )

    own_parts = []

    def finish(step, at, atom, stack):
        part = second_step(atom, stack)
        if step == 3:
            own_parts.append(part)
            return
        send_buf[step, at] = part.astype(BF16)
        if at == 3:
            part_copy(step).start()

    waiting = None
    for step in range(4):
        for at in range(4):
            atom = 4 * target(step) + at
            stack = first_step(atom)
            if waiting is not None:
                finish(*waiting)
            waiting = (step, at, atom, stack)
    finish(*waiting)

    part_copy(2).wait_recv()
    sums = [own_parts[at] + recv_buf[2, at].astype(F32) for at in range(4)]
    part_copy(0).wait_recv()
    part_copy(1).wait_recv()
    for at in range(4):
        total = sums[at] + recv_buf[0, at].astype(F32) + recv_buf[1, at].astype(F32)
        for turn in range(4):
            turned[turn, at * 36 : at * 36 + NO, :] = pltpu.roll(total, NO * turn, 1) if turn else total
    for g in range(4):
        for high in range(8):
            value = None
            for low in range(4):
                line = turned[(low - g) % 4, pl.ds(high * 4 + low, 4, stride=36), :]
                value = line if value is None else jnp.where(masks[low][:4], line, value)
            start = (g % 2 * 8 + high) * 128
            out[g // 2, :, start : start + 128] = value

    for eps in range(4):
        @pl.when(inside(-2))
        def _():
            down(eps).wait_send()

        @pl.when(inside(2))
        def _():
            up(eps).wait_send()

        across_pair(eps).wait_send()

        @pl.when(passing)
        def _():
            forward(eps).wait_send()

    for step in range(3):
        part_copy(step).wait_send()


def body(green, coupling, gradient, neighbours, offsets):
    count, natoms = green.shape[1], green.shape[2]
    anywhere = pl.BlockSpec(memory_space=pl.ANY)
    vmem = pltpu.VMEM
    dma = pltpu.SemaphoreType.DMA
    return pl.pallas_call(
        kernel,
        out_shape=pltpu.VMEM((count, natoms // 4, 2 * NO * NO), F32),
        in_specs=[anywhere] * 5,
        out_specs=pl.BlockSpec(memory_space=vmem),
        scratch_shapes=[
            vmem((2, NA, 2048), BF16),
            vmem((4, 2, NA, 2048), BF16),
            vmem((ROWS, 1024), BF16),
            vmem((NS * 9, NB, 1, NA), F32),
            pltpu.SMEM((NB, NA), jnp.int32),
            pltpu.SMEM((NW,), jnp.int32),
            vmem((NS * 9, 8, 128), F32),
            vmem((NO * STEP, 128), F32),
            vmem((NA, 24, 8, 128), F32),
            vmem((512, 128), F32),
            vmem((NA, NB, 256, 128), BF16),
            vmem((NA, NO, 512), BF16),
            vmem((4, 64 * GAP, 128), F32),
            vmem((NA, 128, 256), BF16),
            vmem((3, 4, NO, 128), BF16),
            vmem((3, 4, NO, 128), BF16),
            vmem((4, 4 * 36, 128), F32),
            dma((5,)),
            dma((4, 4)),
            dma((4, 4)),
            dma((3,)),
            dma((3,)),
        ],
        compiler_params=pltpu.CompilerParams(collective_id=0, has_side_effects=True),
    )(
        green[0],
        coupling.reshape(NS * 9, NB, 1, NA),
        gradient.reshape(ROWS, NO * NO),
        neighbours.T,
        offsets,
    )


def solution(mesh):
    in_specs = (P("mom", "energy", None, None), P("mom", None, None, None, None), P(), P(), P())
    out_specs = P("energy", "mom", None)
    return jax.shard_map(body, mesh=mesh, in_specs=in_specs, out_specs=out_specs, check_vma=False)
```

```python
import jax
import jax.numpy as jnp
from jax import lax
from jax.experimental import pallas as pl
from jax.experimental.pallas import tpu as pltpu
from jax.sharding import PartitionSpec as P

NO = 32
NB = 5
NW = 3
NA = 16
NS = 2 * NW
ROWS = NB * 3 * NA
STEP = 68
GAP = 20
STOPS = (0, 0, 2, 3)
MESH = pl.DeviceIdType.MESH
F32 = jnp.float32
BF16 = jnp.bfloat16
SHIFTS = (-2, -1, 1, 2)


def lane_group(rows, lanes=128):
    return lax.broadcasted_iota(jnp.int32, (rows, lanes), 1) // NO


def kernel(
    green, coupling, gradient, neighbours, offsets, out,
    own, halo, grad_v, coup_v, near, offs,
    coup_rows, spread, coef, flipped, kern, derivs, wide, blocks, send_buf, recv_buf, turned,
    local_sem, halo_send, halo_recv, part_send, part_recv,
):
    n_energy = lax.axis_size("energy")
    energy = lax.axis_index("energy")
    mom = lax.axis_index("mom")

    loads = [
        pltpu.make_async_copy(gradient, grad_v, local_sem.at[0]),
        pltpu.make_async_copy(coupling, coup_v, local_sem.at[1]),
        pltpu.make_async_copy(offsets, offs, local_sem.at[2]),
        pltpu.make_async_copy(green, own, local_sem.at[3]),
        pltpu.make_async_copy(neighbours, near, local_sem.at[4]),
    ]

    def inside(by):
        return jnp.logical_and(energy + by >= 0, energy + by < n_energy)

    barrier = pltpu.get_barrier_semaphore()
    odd = lax.rem(energy, 2)
    mate = energy + 1 - 2 * odd
    for by in (-2, 2):
        @pl.when(inside(by))
        def _():
            pl.semaphore_signal(barrier, inc=1, device_id={"energy": energy + by}, device_id_type=MESH)
    pl.semaphore_signal(barrier, inc=1, device_id={"energy": mate}, device_id_type=MESH)
    for step in range(1, 4):
        pl.semaphore_signal(barrier, inc=1, device_id={"mom": lax.rem(mom + step, 4)}, device_id_type=MESH)
    for load in loads:
        load.start()
    expected = 4
    for by in (-2, 2):
        expected = expected + inside(by).astype(jnp.int32)

    pl.semaphore_wait(barrier, expected)

    def halo_copy(source, eps, slot, kind, peer):
        return pltpu.make_async_remote_copy(
            src_ref=source.at[eps // 2, :, eps % 2 * 1024 : eps % 2 * 1024 + 1024],
            dst_ref=halo.at[slot, eps // 2, :, eps % 2 * 1024 : eps % 2 * 1024 + 1024],
            send_sem=halo_send.at[kind, eps],
            recv_sem=halo_recv.at[slot, eps],
            device_id={"energy": peer},
            device_id_type=MESH,
        )

    def up(eps):
        return halo_copy(green, eps, 0, 0, energy + 2)

    def down(eps):
        return halo_copy(green, eps, 3, 1, energy - 2)

    def across_pair(eps):
        return halo_copy(green, eps, 1 + odd, 2, mate)

    def forward(eps):
        return halo_copy(halo.at[3 - 3 * odd], eps, 2 - odd, 3, mate)

    def arrived(slot, eps):
        halo_copy(green, eps, slot, 0, mate).wait_recv()

    passing = jnp.logical_or(jnp.logical_and(odd == 0, inside(2)), jnp.logical_and(odd == 1, inside(-2)))
    for eps in range(4):
        @pl.when(inside(-2))
        def _():
            down(eps).start()

        @pl.when(inside(2))
        def _():
            up(eps).start()

        across_pair(eps).start()
    for slot in range(4):
        @pl.when(jnp.logical_not(inside(SHIFTS[slot])))
        def _():
            halo[slot] = jnp.zeros(halo.shape[1:], BF16)

    col = lax.broadcasted_iota(jnp.int32, (1, 512), 1)
    wanted = (col // NO) % 4 * 128 + col // 128 * NO + col % NO
    rows = lax.broadcasted_iota(jnp.int32, (512, 512), 0)
    pick = jnp.where(rows == wanted, 1.0, 0.0).astype(BF16)
    loads[0].wait()
    lines = []
    for chunk in range(8):
        tiles = []
        for g in range(4):
            parts = []
            for tile in range(4):
                block = 4 * tile + g
                if block < 3 * NB:
                    parts.append(grad_v[block * NA : (block + 1) * NA, chunk * 128 : (chunk + 1) * 128])
                else:
                    parts.append(jnp.zeros((NA, 128), BF16))
            tiles.append(jnp.concatenate(parts, axis=0))
        lines.append(jnp.concatenate(tiles, axis=1))
    packed = jnp.dot(jnp.concatenate(lines, axis=0), pick, preferred_element_type=F32)
    for chunk in range(8):
        for q in range(4):
            start = (chunk * 4 + q) * STEP
            spread[start : start + 64, :] = packed[chunk * 64 : (chunk + 1) * 64, q * 128 : (q + 1) * 128]

    loads[1].wait()
    loads[2].wait()

    for pair in range(NS * 9):
        for slot in range(NB):
            coup_rows[pair, slot : slot + 1, :NA] = coup_v[pair, slot]
    group8 = lane_group(8)
    weights = [
        [jnp.broadcast_to(jnp.where(offs[w] == size, 1.0, 0.0), (8, 128)) for w in range(NW)] for size in range(1, 5)
    ]

    def coef_step(j, carry):
        tables = [[coup_rows[s * 9 + 3 * i + j] for i in range(3)] for s in range(NS)]
        for atom in range(NA):
            terms = []
            for s in range(NS):
                first, second, third = [
                    jnp.broadcast_to(tables[s][i][:, atom : atom + 1], (8, 128)) for i in range(3)
                ]
                terms.append(jnp.where(group8 == 0, first, jnp.where(group8 == 1, second, third)))
            for size in range(1, 5):
                for g in range(2):
                    k = 4 * g + size - 1
                    total = None
                    for w in range(NW):
                        term = weights[size - 1][w] * terms[2 * w + g]
                        total = term if total is None else total + term
                    coef[atom, k * 3 + j] = total
        return carry

    lax.fori_loop(0, 3, coef_step, 0)

    def make_kernels(atom, carry):
        for tile in range(4):
            block = spread[pl.ds(tile * NA + atom, NO, stride=STEP), :]
            derivs[atom, :, tile * 128 : (tile + 1) * 128] = block.astype(BF16)
            flipped[tile * 128 : (tile + 1) * 128, :] = jnp.concatenate([block] * 4, axis=0).T
        for slot in range(NB):
            d = [flipped[(slot * 3 + j) * NO : (slot * 3 + j + 1) * NO, :] for j in range(3)]
            for k in range(8):
                total = None
                for j in range(3):
                    line = coef[atom, k * 3 + j, slot : slot + 1, :]
                    term = jnp.broadcast_to(line, (NO, 128)) * d[j]
                    total = term if total is None else total + term
                kern[atom, slot, k * NO : (k + 1) * NO, :] = total.astype(BF16)
        return carry

    def pass_on(eps):
        @pl.when(passing)
        def _():
            arrived(3 - 3 * odd, eps)
            forward(eps).start()

    done = 0
    for eps, stop in enumerate(STOPS):
        if stop > done:
            lax.fori_loop(done, stop, make_kernels, 0)
        done = stop
        pass_on(eps)
    lax.fori_loop(done, NA, make_kernels, 0)

    group16 = lane_group(NA)

    masks16 = [group16 == g for g in range(4)]

    def arrive(slot):
        @pl.when(inside(SHIFTS[slot]))
        def _():
            for eps in range(4):
                arrived(slot, eps)

    def place(half):
        def chunk_step(chunk, carry):
            lanes = pl.ds(pl.multiple_of(chunk * 128, 128), 128)
            turns = {}
            for e in range(2):
                for at in range(4):
                    row = e - (at + 1) * (1 - 2 * half)
                    if row not in turns:
                        block, eps = row // 2, row % 2
                        tile = own[eps, :, lanes] if block == 0 else halo[SHIFTS.index(block), eps, :, lanes]
                        turns[row] = [tile] + [pltpu.roll(tile, NO * k, 1) for k in range(1, 4)]
            for e in range(2):
                for q in range(4):
                    value = None
                    for at in range(4):
                        part = turns[e - (at + 1) * (1 - 2 * half)][(at - q) % 4]
                        value = part if value is None else jnp.where(masks16[at], part, value)
                    start = pl.multiple_of((chunk * 4 + q) * GAP, 4)
                    wide[e * 2 + half, pl.ds(start, NA), :] = value.astype(F32)
            return carry

        lax.fori_loop(0, 16, chunk_step, 0, unroll=8)

        def gather_atom(atom, carry):
            for e in range(2):
                part = wide[e * 2 + half, pl.ds(atom, 2 * NO, stride=GAP), :]
                blocks[atom, e * 64 : (e + 1) * 64, half * 128 : (half + 1) * 128] = part.astype(BF16)
            return carry

        lax.fori_loop(0, NA, gather_atom, 0, unroll=8)

    loads[3].wait()
    @pl.when(odd == 0)
    def _():
        arrive(2)
        place(1)
        arrive(0)
        arrive(1)
        place(0)

    @pl.when(odd == 1)
    def _():
        arrive(1)
        place(0)
        arrive(3)
        arrive(2)
        place(1)

    loads[4].wait()

    group = lane_group(NO)
    masks = [group == g for g in range(4)]

    def first_step(atom):
        stack = []
        for slot in range(NB):
            middle = jnp.dot(blocks[near[slot, atom]], kern[atom, slot], preferred_element_type=F32).astype(BF16)
            parts = [middle[g * NO : (g + 1) * NO, :] for g in range(4)]
            for i in range(3):
                value = None
                for g in range(4):
                    turn = (g - i) % 4
                    part = pltpu.roll(parts[g], NO * turn, 1) if turn else parts[g]
                    value = part if value is None else jnp.where(masks[g], part, value)
                stack.append(value)
        stack.append(jnp.zeros((NO, 128), BF16))
        return jnp.concatenate(stack, axis=0)

    def second_step(atom, stack):
        return jnp.dot(derivs[atom], stack, preferred_element_type=F32)

    def target(step):
        high = lax.rem(mom // 2 + 1 - step // 2, 2)
        low = lax.rem(mom + (step + 1) // 2, 2)
        return 2 * high + low

    def part_copy(step):
        return pltpu.make_async_remote_copy(
            src_ref=send_buf.at[step],
            dst_ref=recv_buf.at[step],
            send_sem=part_send.at[step],
            recv_sem=part_recv.at[step],
            device_id={"mom": target(step)},
            device_id_type=MESH,
        )

    own_parts = []

    def finish(step, at, atom, stack):
        part = second_step(atom, stack)
        if step == 3:
            own_parts.append(part)
            return
        send_buf[step, at] = part.astype(BF16)
        if at == 3:
            part_copy(step).start()

    waiting = None
    for step in range(4):
        for at in range(4):
            atom = 4 * target(step) + at
            stack = first_step(atom)
            if waiting is not None:
                finish(*waiting)
            waiting = (step, at, atom, stack)
    finish(*waiting)

    part_copy(2).wait_recv()
    sums = [own_parts[at] + recv_buf[2, at].astype(F32) for at in range(4)]
    part_copy(0).wait_recv()
    part_copy(1).wait_recv()
    for at in range(4):
        total = sums[at] + recv_buf[0, at].astype(F32) + recv_buf[1, at].astype(F32)
        for turn in range(4):
            turned[turn, at * 36 : at * 36 + NO, :] = pltpu.roll(total, NO * turn, 1) if turn else total
    for g in range(4):
        for high in range(8):
            value = None
            for low in range(4):
                line = turned[(low - g) % 4, pl.ds(high * 4 + low, 4, stride=36), :]
                value = line if value is None else jnp.where(masks[low][:4], line, value)
            start = (g % 2 * 8 + high) * 128
            out[g // 2, :, start : start + 128] = value

    for eps in range(4):
        @pl.when(inside(-2))
        def _():
            down(eps).wait_send()

        @pl.when(inside(2))
        def _():
            up(eps).wait_send()

        across_pair(eps).wait_send()

        @pl.when(passing)
        def _():
            forward(eps).wait_send()

    for step in range(3):
        part_copy(step).wait_send()


def body(green, coupling, gradient, neighbours, offsets):
    count, natoms = green.shape[1], green.shape[2]
    anywhere = pl.BlockSpec(memory_space=pl.ANY)
    vmem = pltpu.VMEM
    dma = pltpu.SemaphoreType.DMA
    return pl.pallas_call(
        kernel,
        out_shape=pltpu.VMEM((count, natoms // 4, 2 * NO * NO), F32),
        in_specs=[anywhere] * 5,
        out_specs=pl.BlockSpec(memory_space=vmem),
        scratch_shapes=[
            vmem((2, NA, 2048), BF16),
            vmem((4, 2, NA, 2048), BF16),
            vmem((ROWS, 1024), BF16),
            vmem((NS * 9, NB, 1, NA), F32),
            pltpu.SMEM((NB, NA), jnp.int32),
            pltpu.SMEM((NW,), jnp.int32),
            vmem((NS * 9, 8, 128), F32),
            vmem((NO * STEP, 128), F32),
            vmem((NA, 24, 8, 128), F32),
            vmem((512, 128), F32),
            vmem((NA, NB, 256, 128), BF16),
            vmem((NA, NO, 512), BF16),
            vmem((4, 64 * GAP, 128), F32),
            vmem((NA, 128, 256), BF16),
            vmem((3, 4, NO, 128), BF16),
            vmem((3, 4, NO, 128), BF16),
            vmem((4, 4 * 36, 128), F32),
            dma((5,)),
            dma((4, 4)),
            dma((4, 4)),
            dma((3,)),
            dma((3,)),
        ],
        compiler_params=pltpu.CompilerParams(collective_id=0, has_side_effects=True),
    )(
        green[0],
        coupling.reshape(NS * 9, NB, 1, NA),
        gradient.reshape(ROWS, NO * NO),
        neighbours.T,
        offsets,
    )


def solution(mesh):
    in_specs = (P("mom", "energy", None, None), P("mom", None, None, None, None), P(), P(), P())
    out_specs = P("energy", "mom", None)
    return jax.shard_map(body, mesh=mesh, in_specs=in_specs, out_specs=out_specs, check_vma=False)
```
